32 devices in a mesh: prow: 8 (over y, x, core), pcol: 4 (over z).
Axes of the slice: x: 2, y: 2, z: 4, core: 2. Of those that a mesh axis runs over, the one named last changes fastest.
Arguments:
- cov_trail: float32 [1024, 1024], P('prow', 'pcol'), as said below
- factor_panel: bfloat16 [4, 1024, 128], P(None, 'prow'), may hold values from -0.25 to 0.25
- first_level: int32 [8], replicated, may hold values from 0 to 4
- block_slot: int32 [8], replicated, may hold values from 0 to 7, each once
- factor_window: bfloat16 [6, 128, 128], replicated, may hold values from -0.5 to 0.5
- diag_inverse: float32 [4, 128, 128], replicated, as said below
Outputs:
- panel_cov: float32 [4, 1024, 128], P(None, 'prow')
- window_cov: float32 [512, 512], replicated
The draws below stay inside these ranges and needn't reach their ends.
Inputs may be any that keep to these rules, and one draw needn't show every extreme that they name: Trailing block j lies in the pattern of window supernode k exactly when first_level[j] <= k, so the patterns are nested. `block_slot`: a permutation; slot s is held by process row s // 1 and process column s // (8 / pcol size), slots in contiguous blocks. `cov_trail`: symmetric. `diag_inverse`: each block symmetric.
All inputs are finite; a program needn't handle non-finite values.
Results may differ from the reference program's by a relative error of at most 0.0003.
Values may be sent and summed in bfloat16 or wider, within the bound.
A program may use at most 64 MiB of HBM per device.

```python
import jax
import jax.numpy as jnp
from jax import lax

BS = 128
NW = 4
NT = 8
ORDER = 1024
NPAIR = 6


def draw_cov_trail(key, part):
    order_size = NT * BS
    noise = jax.random.normal(key, (order_size, order_size), jnp.float32)
    symmetric = (noise + noise.T) * 0.7071
    row_ids = lax.broadcasted_iota(jnp.int32, (order_size, order_size), 0)
    col_ids = lax.broadcasted_iota(jnp.int32, (order_size, order_size), 1)
    on_diag = jnp.where(row_ids == col_ids, jnp.float32(2.0), jnp.float32(0.0))
    return symmetric + on_diag


def draw_diag_inverse(key, part):
    noise = jax.random.normal(key, (NW, BS, BS), jnp.float32) * 0.01
    symmetric = noise + jnp.swapaxes(noise, 1, 2)
    row_ids = lax.broadcasted_iota(jnp.int32, (NW, BS, BS), 1)
    col_ids = lax.broadcasted_iota(jnp.int32, (NW, BS, BS), 2)
    return symmetric + jnp.where(row_ids == col_ids, jnp.float32(2.0), jnp.float32(0.0))


def set_ends(result, stream_key, low, largest):
    longest = result.shape.index(max(result.shape))
    spots = []
    for shift in (0, 1):
        where = [jax.random.randint(jax.random.fold_in(stream_key, axis), (), 0, length) for axis, length in enumerate(result.shape)]
        where[longest] = (where[longest] + shift) % result.shape[longest]
        spots.append(tuple(where))
    return result.at[spots[0]].set(low).at[spots[1]].set(largest)


def block_levels(stream_key, extent, shards, low, largest):
    loudness = 1.0
    for dim, shards_of in shards:
        draws = jax.random.uniform(jax.random.fold_in(jax.random.fold_in(stream_key, 6), dim), (shards_of,), jnp.float32, low / len(shards), largest / len(shards))
        loudness = loudness * jnp.repeat(jnp.exp(draws), extent[dim] // shards_of).reshape((-1,) + (1,) * (len(extent) - 1 - dim))
    return loudness


def gaussian(own_key, dims, deviation, reach, shards=(), kind=jnp.bfloat16):
    entries = deviation * jax.random.normal(own_key, dims, jnp.float32)
    if shards:
        entries = entries * block_levels(own_key, dims, shards, -0.22, 0.18)
    return jnp.clip(entries, -reach, reach).astype(kind)


def setup_inputs(seed: int = 0) -> dict:
    key_of = jax.random.split(jax.random.key(seed), 7)
    cov_trail = draw_cov_trail(jax.random.fold_in(key_of[6], 71), 0)
    factor_panel = gaussian(key_of[1], (NW, ORDER, BS), (64 * NT) ** -0.5, 0.25, ((1, 8),))
    first_level = set_ends(jax.random.randint(key_of[2], (NT,), 0, NW + 1), jax.random.fold_in(key_of[2], 1), 0, NW).astype(jnp.int32)
    block_slot = jax.random.permutation(key_of[3], NT).astype(jnp.int32)
    factor_window = gaussian(key_of[4], (NPAIR, BS, BS), BS ** -0.5, 0.5)
    diag_inverse = draw_diag_inverse(jax.random.fold_in(key_of[6], 71), 0)
    return {"cov_trail": cov_trail, "factor_panel": factor_panel, "first_level": first_level, "block_slot": block_slot, "factor_window": factor_window, "diag_inverse": diag_inverse}


def pair_index(upper, lower, window_count):
    return lower * window_count - lower * (lower + 1) // 2 + upper - lower - 1


def later_block(window, upper, lower):
    if upper >= lower:
        return window[(upper, lower)]
    return window[(lower, upper)].T


def reference(cov_trail, factor_panel, first_level, block_slot, factor_window, diag_inverse):
    highest = lax.Precision.HIGHEST
    slot_ids = jnp.arange(NT, dtype=jnp.int32)
    level_slot = jnp.sum(jnp.where(block_slot[None, :] == slot_ids[:, None], first_level[None, :], 0), axis=1)
    row_level = jnp.repeat(level_slot, BS)
    columns = {}
    window = {}
    for supernode in range(NW - 1, -1, -1):
        keep_rows = (row_level <= supernode)[:, None]
        panel_full = jnp.where(keep_rows, factor_panel[supernode].astype(jnp.float32), jnp.float32(0.0))
        later_nodes = list(range(supernode + 1, NW))
        window_factor = [factor_window[pair_index(upper, supernode, NW)].astype(jnp.float32) for upper in later_nodes]
        accumulated = jnp.dot(cov_trail, panel_full, precision=highest, preferred_element_type=jnp.float32)
        for place, upper in enumerate(later_nodes):
            accumulated = accumulated + jnp.dot(columns[upper], window_factor[place], precision=highest, preferred_element_type=jnp.float32)
        new_column = jnp.where(keep_rows, -accumulated, jnp.float32(0.0))
        columns[supernode] = new_column
        for upper in later_nodes:
            block_total = jnp.dot(columns[upper].T, panel_full, precision=highest, preferred_element_type=jnp.float32)
            for place, other in enumerate(later_nodes):
                block_total = block_total + jnp.dot(later_block(window, upper, other), window_factor[place], precision=highest, preferred_element_type=jnp.float32)
            window[(upper, supernode)] = -block_total
        diagonal = diag_inverse[supernode] - jnp.dot(panel_full.T, new_column, precision=highest, preferred_element_type=jnp.float32)
        for place, upper in enumerate(later_nodes):
            diagonal = diagonal - jnp.dot(window_factor[place].T, window[(upper, supernode)], precision=highest, preferred_element_type=jnp.float32)
        window[(supernode, supernode)] = diagonal
    panel_cov = jnp.stack([columns[supernode] for supernode in range(NW)])
    block_rows = [jnp.concatenate([later_block(window, upper, other) for other in range(NW)], axis=1) for upper in range(NW)]
    window_cov = jnp.concatenate(block_rows, axis=0)
    return panel_cov, window_cov
```

```python
import functools

import jax
import jax.numpy as jnp
from jax import lax
from jax.experimental import pallas as pl
from jax.experimental.pallas import tpu as pltpu
from jax.sharding import PartitionSpec as P

MESH = pl.DeviceIdType.MESH
F32 = jnp.float32
BF16 = jnp.bfloat16


def pair_index(upper, lower, window_count):
    return lower * window_count - lower * (lower + 1) // 2 + upper - lower - 1


def split(value):
    high = value.astype(BF16)
    return high, (value - high.astype(F32)).astype(BF16)


def dot(left, right):
    return jnp.dot(left, right, preferred_element_type=F32)


def kernel(
    sizes,
    first_ref,
    slot_ref,
    cov_ref,
    panel_ref,
    factor_ref,
    diag_ref,
    column_ref,
    window_ref,
    panels,
    masked,
    panel_t,
    factor_t,
    product,
    product_in,
    sums,
    inner,
    inner_in,
    pieces,
    x_parts,
    w_parts,
    panel_send,
    panel_fwd,
    panel_recv,
    product_send,
    product_recv,
    sums_send,
    sums_recv,
    inner_send,
    inner_recv,
    piece_send,
    piece_recv,
    row_send,
    row_fwd,
    row_recv,
):
    n_row, n_col, window_count, block = sizes
    local_blocks = cov_ref.shape[1] // block
    n_chip = n_row // 2
    width = window_count * block
    block_count = first_ref.shape[0]
    row_blocks = cov_ref.shape[0] // block
    chunk = product.shape[2]
    piece_rows = width // n_row
    me = lax.axis_index("prow")
    col = lax.axis_index("pcol")
    core = lax.rem(me, 2)
    chip = me // 2
    partner = chip * 2 + 1 - core

    def remote(src, dst, send, recv, row, column):
        return pltpu.make_async_remote_copy(
            src_ref=src,
            dst_ref=dst,
            send_sem=send,
            recv_sem=recv,
            device_id=(row, column),
            device_id_type=MESH,
        )

    def level_of(slot):
        level = jnp.int32(0)
        for index in range(block_count):
            level = level + jnp.where(slot_ref[index] == slot, first_ref[index], 0)
        return level

    barrier = pltpu.get_barrier_semaphore()
    for step in range(1, n_row):
        pl.semaphore_signal(
            barrier, inc=1, device_id=(lax.rem(me + step, n_row), col), device_id_type=MESH
        )
    for step in range(1, n_col):
        pl.semaphore_signal(
            barrier, inc=1, device_id=(me, lax.rem(col + step, n_col)), device_id_type=MESH
        )
    pl.semaphore_wait(barrier, n_row + n_col - 2)

    for turn in range(local_blocks // 2):
        mine = 2 * turn + core
        owner = col * local_blocks + mine

        @pl.when(me == owner)
        def _():
            for step in range(1, n_chip):
                target = lax.rem(chip + step, n_chip) * 2 + core
                remote(
                    panel_ref, panels.at[mine], panel_send.at[turn, step], panel_recv.at[mine], target, col
                ).start()
            remote(
                panel_ref, panels.at[mine], panel_fwd.at[turn], panel_recv.at[mine], partner, col
            ).start()
            panels[mine] = panel_ref[...]

    own_level = level_of(me)
    for k in range(window_count):
        own = jnp.where(own_level <= k, panel_ref[k].astype(F32), 0.0)
        panel_t[pl.ds(k * block, block), :] = own.T.astype(BF16)
    for index in range(factor_ref.shape[0]):
        factor_t[index] = factor_ref[index].astype(F32).T.astype(BF16)
    cov_high, cov_low = split(cov_ref[...])
    cov_parts = jnp.concatenate([cov_high, cov_low], axis=0)

    for turn in range(local_blocks // 2):
        mine = 2 * turn + core
        owner = col * local_blocks + mine

        @pl.when(me != owner)
        def _():
            forward = remote(
                panels.at[mine], panels.at[mine], panel_fwd.at[turn], panel_recv.at[mine], partner, col
            )
            forward.wait_recv()
            forward.start()

    for turn in range(local_blocks // 2):
        other = 2 * turn + 1 - core
        remote(
            panels.at[other], panels.at[other], panel_fwd.at[turn], panel_recv.at[other], partner, col
        ).wait_recv()

    for index in range(local_blocks):
        level = level_of(col * local_blocks + index)
        for k in range(window_count):
            masked[pl.ds(index * block, block), pl.ds(k * block, block)] = jnp.where(
                level <= k, panels[index, k].astype(F32), 0.0
            ).astype(BF16)

    rows = cov_ref.shape[0]
    both = dot(cov_parts, masked[...])
    partial = both[:rows] + both[rows:]
    for index in range(n_col):
        product[index] = partial[:, index * chunk : (index + 1) * chunk]
    for step in range(1, n_col):
        target = lax.rem(col + step, n_col)
        remote(
            product.at[target], product_in.at[col], product_send.at[step], product_recv.at[col], me, target
        ).start()
    total = product[col]
    for step in range(1, n_col):
        source = lax.rem(col + step, n_col)
        remote(
            product.at[source], product_in.at[source], product_send.at[step], product_recv.at[source], me, source
        ).wait_recv()
        total = total + product_in[source]
    sums[col] = total

    high, low = split(total)
    inner_both = dot(panel_t[...], jnp.concatenate([high, low], axis=1))
    inner_sum = inner_both[:, :chunk] + inner_both[:, chunk:]
    for index in range(n_row):
        inner[index] = inner_sum[index * piece_rows : (index + 1) * piece_rows]
    for step in range(1, n_row):
        target = lax.rem(me + step, n_row)
        remote(
            inner.at[target], inner_in.at[me], inner_send.at[step], inner_recv.at[me], target, col
        ).start()
    for step in range(1, n_col):
        target = lax.rem(col + step, n_col)
        remote(
            sums.at[col], sums.at[col], sums_send.at[step], sums_recv.at[col], me, target
        ).start()
    piece = inner[me]
    for step in range(1, n_row):
        source = lax.rem(me + step, n_row)
        remote(
            inner.at[source], inner_in.at[source], inner_send.at[step], inner_recv.at[source], source, col
        ).wait_recv()
        piece = piece + inner_in[source]
    pieces[me, col] = piece
    for step in range(1, n_col):
        target = lax.rem(col + step, n_col)
        remote(
            pieces.at[me, col], pieces.at[me, col], piece_send.at[step], piece_recv.at[col], me, target
        ).start()
    for step in range(1, n_col):
        source = lax.rem(col + step, n_col)
        remote(
            pieces.at[me, source], pieces.at[me, source], piece_send.at[step], piece_recv.at[source], me, source
        ).wait_recv()
    for step in range(1, n_chip):
        target = lax.rem(chip + step, n_chip) * 2 + core
        remote(
            pieces.at[me], pieces.at[me], row_send.at[step], row_recv.at[me], target, col
        ).start()
    remote(pieces.at[me], pieces.at[me], row_fwd.at[chip], row_recv.at[me], partner, col).start()

    for step in range(1, n_col):
        source = lax.rem(col + step, n_col)
        remote(
            sums.at[source], sums.at[source], sums_send.at[step], sums_recv.at[source], me, source
        ).wait_recv()
    full = jnp.concatenate([sums[index] for index in range(n_col)], axis=1)
    done_high, done_low = {}, {}
    for k in range(window_count - 1, -1, -1):
        value = full[:, k * block : (k + 1) * block]
        later = range(k + 1, window_count)
        if k + 1 < window_count:
            factor = jnp.concatenate(
                [factor_ref[pair_index(w, k, window_count)] for w in later], axis=0
            )
            left = jnp.concatenate(
                [
                    jnp.concatenate([done_high[w] for w in later], axis=1),
                    jnp.concatenate([done_low[w] for w in later], axis=1),
                ],
                axis=0,
            )
            term = dot(left, factor)
            value = value + (term[:rows] + term[rows:])
        value = -value
        done_high[k], done_low[k] = split(value)
        column_ref[k] = jnp.where(own_level <= k, value, 0.0)

    for step in range(1, n_chip):
        source = lax.rem(chip + step, n_chip)
        row = source * 2 + core
        forward = remote(
            pieces.at[row], pieces.at[row], row_fwd.at[source], row_recv.at[row], partner, col
        )
        forward.wait_recv()
        forward.start()
    for source in range(n_chip):
        row = source * 2 + 1 - core
        remote(
            pieces.at[row], pieces.at[row], row_fwd.at[source], row_recv.at[row], partner, col
        ).wait_recv()

    known = jnp.concatenate(
        [
            jnp.concatenate([pieces[row, index] for index in range(n_col)], axis=1)
            for row in range(n_row)
        ],
        axis=0,
    )
    for k in range(window_count - 1, -1, -1):
        start = k * block
        value = known[:, start : start + block]
        zero = jnp.zeros((block, block), F32)
        value = value + jnp.concatenate(
            [diag_ref[k] if w == k else zero for w in range(window_count)], axis=0
        )
        if k + 1 < window_count:
            factor = jnp.concatenate(
                [factor_ref[pair_index(w, k, window_count)] for w in range(k + 1, window_count)],
                axis=0,
            )
            after = pl.ds(start + block, width - start - block)
            value = value - (dot(x_parts[0, :, after], factor) + dot(x_parts[1, :, after], factor))
        high, low = split(value)
        x_parts[0, :, pl.ds(start, block)] = high
        x_parts[1, :, pl.ds(start, block)] = low
        window_ref[:, pl.ds(start, block)] = value
    for k in range(window_count - 1, -1, -1):
        start = k * block
        value = window_ref[pl.ds(start, block), :]
        if k + 1 < window_count:
            factor = jnp.concatenate(
                [factor_t[pair_index(w, k, window_count)] for w in range(k + 1, window_count)],
                axis=1,
            )
            after = pl.ds(start + block, width - start - block)
            value = value - (dot(factor, w_parts[0, after, :]) + dot(factor, w_parts[1, after, :]))
            window_ref[pl.ds(start, block), :] = value
        high, low = split(value)
        w_parts[0, pl.ds(start, block), :] = high
        w_parts[1, pl.ds(start, block), :] = low

    for turn in range(local_blocks // 2):
        mine = 2 * turn + core

        @pl.when(me == col * local_blocks + mine)
        def _():
            for step in range(1, n_chip):
                remote(
                    panel_ref, panels.at[mine], panel_send.at[turn, step], panel_recv.at[mine], partner, col
                ).wait_send()

        remote(
            panels.at[mine], panels.at[mine], panel_fwd.at[turn], panel_recv.at[mine], partner, col
        ).wait_send()
    for step in range(1, n_col):
        remote(
            product.at[col], product_in.at[col], product_send.at[step], product_recv.at[col], me, col
        ).wait_send()
        remote(sums.at[col], sums.at[col], sums_send.at[step], sums_recv.at[col], me, col).wait_send()
        remote(
            pieces.at[me, col], pieces.at[me, col], piece_send.at[step], piece_recv.at[col], me, col
        ).wait_send()
    for step in range(1, n_row):
        remote(
            inner.at[me], inner_in.at[me], inner_send.at[step], inner_recv.at[me], partner, col
        ).wait_send()
    for step in range(1, n_chip):
        remote(pieces.at[me], pieces.at[me], row_send.at[step], row_recv.at[me], partner, col).wait_send()
    for source in range(n_chip):
        remote(
            pieces.at[me], pieces.at[me], row_fwd.at[source], row_recv.at[me], partner, col
        ).wait_send()


def solution(mesh):
    n_row, n_col = mesh.shape["prow"], mesh.shape["pcol"]

    def shards(cov_trail, factor_panel, first_level, block_slot, factor_window, diag_inverse):
        window_count, block = diag_inverse.shape[0], diag_inverse.shape[-1]
        rows, cols = cov_trail.shape
        width = window_count * block
        chunk = width // n_col
        piece = width // n_row
        local_blocks = cols // block
        pairs = factor_window.shape[0]
        vmem = pl.BlockSpec(memory_space=pltpu.VMEM)
        smem = pl.BlockSpec(memory_space=pltpu.SMEM)
        dma = pltpu.SemaphoreType.DMA
        return pl.pallas_call(
            functools.partial(kernel, (n_row, n_col, window_count, block)),
            out_shape=(
                jax.ShapeDtypeStruct((window_count, rows, block), F32),
                jax.ShapeDtypeStruct((width, width), F32),
            ),
            in_specs=[smem, smem, vmem, vmem, vmem, vmem],
            out_specs=(vmem, vmem),
            scratch_shapes=[
                pltpu.VMEM((local_blocks, window_count, block, block), BF16),
                pltpu.VMEM((cols, width), BF16),
                pltpu.VMEM((width, rows), BF16),
                pltpu.VMEM((pairs, block, block), BF16),
                pltpu.VMEM((n_col, rows, chunk), F32),
                pltpu.VMEM((n_col, rows, chunk), F32),
                pltpu.VMEM((n_col, rows, chunk), F32),
                pltpu.VMEM((n_row, piece, chunk), F32),
                pltpu.VMEM((n_row, piece, chunk), F32),
                pltpu.VMEM((n_row, n_col, piece, chunk), F32),
                pltpu.VMEM((2, width, width), BF16),
                pltpu.VMEM((2, width, width), BF16),
                dma((local_blocks // 2, n_row // 2)),
                dma((local_blocks // 2,)),
                dma((local_blocks,)),
                dma((n_col,)),
                dma((n_col,)),
                dma((n_col,)),
                dma((n_col,)),
                dma((n_row,)),
                dma((n_row,)),
                dma((n_col,)),
                dma((n_col,)),
                dma((n_row // 2,)),
                dma((n_row // 2,)),
                dma((n_row,)),
            ],
            compiler_params=pltpu.CompilerParams(
                collective_id=0, has_side_effects=True, vmem_limit_bytes=40 * 1024 * 1024
            ),
        )(first_level, block_slot, cov_trail, factor_panel, factor_window, diag_inverse)

    return jax.shard_map(
        shards,
        mesh=mesh,
        in_specs=(P("prow", "pcol"), P(None, "prow", None), P(), P(), P(), P()),
        out_specs=(P(None, "prow", None), P()),
        check_vma=False,
    )
```

```python
import functools

import jax
import jax.numpy as jnp
from jax import lax
from jax.experimental import pallas as pl
from jax.experimental.pallas import tpu as pltpu
from jax.sharding import PartitionSpec as P

MESH = pl.DeviceIdType.MESH
F32 = jnp.float32
BF16 = jnp.bfloat16


def pair_index(upper, lower, window_count):
    return lower * window_count - lower * (lower + 1) // 2 + upper - lower - 1


def split(value):
    high = value.astype(BF16)
    return high, (value - high.astype(F32)).astype(BF16)


def dot(left, right):
    return jnp.dot(left, right, preferred_element_type=F32)


def kernel(
    sizes,
    first_hbm,
    slot_hbm,
    cov_hbm,
    panel_hbm,
    factor_hbm,
    diag_hbm,
    column_ref,
    window_ref,
    first_ref,
    slot_ref,
    cov_ref,
    panel_ref,
    factor_ref,
    diag_ref,
    load_sem,
    panels,
    masked,
    panel_t,
    factor_t,
    product,
    product_in,
    sums,
    inner,
    inner_in,
    pieces,
    x_parts,
    w_parts,
    panel_send,
    panel_fwd,
    panel_recv,
    product_send,
    product_recv,
    sums_send,
    sums_recv,
    inner_send,
    inner_recv,
    piece_send,
    piece_recv,
    row_send,
    row_fwd,
    row_recv,
):
    n_row, n_col, window_count, block = sizes
    local_blocks = cov_ref.shape[1] // block
    n_chip = n_row // 2
    width = window_count * block
    block_count = first_ref.shape[0]
    row_blocks = cov_ref.shape[0] // block
    chunk = product.shape[2]
    piece_rows = width // n_row
    me = lax.axis_index("prow")
    col = lax.axis_index("pcol")
    core = lax.rem(me, 2)
    chip = me // 2
    partner = chip * 2 + 1 - core

    def remote(src, dst, send, recv, row, column):
        return pltpu.make_async_remote_copy(
            src_ref=src,
            dst_ref=dst,
            send_sem=send,
            recv_sem=recv,
            device_id=(row, column),
            device_id_type=MESH,
        )

    def level_of(slot):
        level = jnp.int32(0)
        for index in range(block_count):
            level = level + jnp.where(slot_ref[index] == slot, first_ref[index], 0)
        return level

    loads = [
        pltpu.make_async_copy(source, target, load_sem.at[index])
        for index, (source, target) in enumerate(
            (
                (panel_hbm, panel_ref),
                (first_hbm, first_ref),
                (slot_hbm, slot_ref),
                (cov_hbm, cov_ref),
                (factor_hbm, factor_ref),
                (diag_hbm, diag_ref),
            )
        )
    ]
    for load in loads:
        load.start()
    barrier = pltpu.get_barrier_semaphore()
    for step in range(1, n_row):
        pl.semaphore_signal(
            barrier, inc=1, device_id=(lax.rem(me + step, n_row), col), device_id_type=MESH
        )
    for step in range(1, n_col):
        pl.semaphore_signal(
            barrier, inc=1, device_id=(me, lax.rem(col + step, n_col)), device_id_type=MESH
        )
    pl.semaphore_wait(barrier, n_row + n_col - 2)
    loads[0].wait()

    for turn in range(local_blocks // 2):
        mine = 2 * turn + core
        owner = col * local_blocks + mine

        @pl.when(me == owner)
        def _():
            for step in range(1, n_chip):
                target = lax.rem(chip + step, n_chip) * 2 + core
                remote(
                    panel_ref, panels.at[mine], panel_send.at[turn, step], panel_recv.at[mine], target, col
                ).start()
            remote(
                panel_ref, panels.at[mine], panel_fwd.at[turn], panel_recv.at[mine], partner, col
            ).start()
            panels[mine] = panel_ref[...]

    loads[1].wait()
    loads[2].wait()
    own_level = level_of(me)
    for k in range(window_count):
        own = jnp.where(own_level <= k, panel_ref[k].astype(F32), 0.0)
        panel_t[pl.ds(k * block, block), :] = own.T.astype(BF16)
    loads[4].wait()
    for index in range(factor_ref.shape[0]):
        factor_t[index] = factor_ref[index].astype(F32).T.astype(BF16)
    loads[3].wait()
    cov_high, cov_low = split(cov_ref[...])
    cov_parts = jnp.concatenate([cov_high, cov_low], axis=0)

    for turn in range(local_blocks // 2):
        mine = 2 * turn + core
        owner = col * local_blocks + mine

        @pl.when(me != owner)
        def _():
            forward = remote(
                panels.at[mine], panels.at[mine], panel_fwd.at[turn], panel_recv.at[mine], partner, col
            )
            forward.wait_recv()
            forward.start()

    for turn in range(local_blocks // 2):
        other = 2 * turn + 1 - core
        remote(
            panels.at[other], panels.at[other], panel_fwd.at[turn], panel_recv.at[other], partner, col
        ).wait_recv()

    for index in range(local_blocks):
        level = level_of(col * local_blocks + index)
        for k in range(window_count):
            masked[pl.ds(index * block, block), pl.ds(k * block, block)] = jnp.where(
                level <= k, panels[index, k].astype(F32), 0.0
            ).astype(BF16)

    rows = cov_ref.shape[0]
    both = dot(cov_parts, masked[...])
    partial = both[:rows] + both[rows:]
    for index in range(n_col):
        product[index] = partial[:, index * chunk : (index + 1) * chunk]
    for step in range(1, n_col):
        target = lax.rem(col + step, n_col)
        remote(
            product.at[target], product_in.at[col], product_send.at[step], product_recv.at[col], me, target
        ).start()
    total = product[col]
    for step in range(1, n_col):
        source = lax.rem(col + step, n_col)
        remote(
            product.at[source], product_in.at[source], product_send.at[step], product_recv.at[source], me, source
        ).wait_recv()
        total = total + product_in[source]
    sums[col] = total

    high, low = split(total)
    inner_both = dot(panel_t[...], jnp.concatenate([high, low], axis=1))
    inner_sum = inner_both[:, :chunk] + inner_both[:, chunk:]
    for index in range(n_row):
        inner[index] = inner_sum[index * piece_rows : (index + 1) * piece_rows]
    for step in range(1, n_row):
        target = lax.rem(me + step, n_row)
        remote(
            inner.at[target], inner_in.at[me], inner_send.at[step], inner_recv.at[me], target, col
        ).start()
    for step in range(1, n_col):
        target = lax.rem(col + step, n_col)
        remote(
            sums.at[col], sums.at[col], sums_send.at[step], sums_recv.at[col], me, target
        ).start()
    piece = inner[me]
    for step in range(1, n_row):
        source = lax.rem(me + step, n_row)
        remote(
            inner.at[source], inner_in.at[source], inner_send.at[step], inner_recv.at[source], source, col
        ).wait_recv()
        piece = piece + inner_in[source]
    pieces[me, col] = piece
    for step in range(1, n_col):
        target = lax.rem(col + step, n_col)
        remote(
            pieces.at[me, col], pieces.at[me, col], piece_send.at[step], piece_recv.at[col], me, target
        ).start()
    for step in range(1, n_col):
        source = lax.rem(col + step, n_col)
        remote(
            pieces.at[me, source], pieces.at[me, source], piece_send.at[step], piece_recv.at[source], me, source
        ).wait_recv()
    for step in range(1, n_chip):
        target = lax.rem(chip + step, n_chip) * 2 + core
        remote(
            pieces.at[me], pieces.at[me], row_send.at[step], row_recv.at[me], target, col
        ).start()
    remote(pieces.at[me], pieces.at[me], row_fwd.at[chip], row_recv.at[me], partner, col).start()

    for step in range(1, n_col):
        source = lax.rem(col + step, n_col)
        remote(
            sums.at[source], sums.at[source], sums_send.at[step], sums_recv.at[source], me, source
        ).wait_recv()
    full = jnp.concatenate([sums[index] for index in range(n_col)], axis=1)
    done_high, done_low = {}, {}
    for k in range(window_count - 1, -1, -1):
        value = full[:, k * block : (k + 1) * block]
        later = range(k + 1, window_count)
        if k + 1 < window_count:
            factor = jnp.concatenate(
                [factor_ref[pair_index(w, k, window_count)] for w in later], axis=0
            )
            left = jnp.concatenate(
                [
                    jnp.concatenate([done_high[w] for w in later], axis=1),
                    jnp.concatenate([done_low[w] for w in later], axis=1),
                ],
                axis=0,
            )
            term = dot(left, factor)
            value = value + (term[:rows] + term[rows:])
        value = -value
        done_high[k], done_low[k] = split(value)
        column_ref[k] = jnp.where(own_level <= k, value, 0.0)

    for step in range(1, n_chip):
        source = lax.rem(chip + step, n_chip)
        row = source * 2 + core
        forward = remote(
            pieces.at[row], pieces.at[row], row_fwd.at[source], row_recv.at[row], partner, col
        )
        forward.wait_recv()
        forward.start()
    for source in range(n_chip):
        row = source * 2 + 1 - core
        remote(
            pieces.at[row], pieces.at[row], row_fwd.at[source], row_recv.at[row], partner, col
        ).wait_recv()

    loads[5].wait()
    known = jnp.concatenate(
        [
            jnp.concatenate([pieces[row, index] for index in range(n_col)], axis=1)
            for row in range(n_row)
        ],
        axis=0,
    )
    for k in range(window_count - 1, -1, -1):
        start = k * block
        value = known[:, start : start + block]
        zero = jnp.zeros((block, block), F32)
        value = value + jnp.concatenate(
            [diag_ref[k] if w == k else zero for w in range(window_count)], axis=0
        )
        if k + 1 < window_count:
            factor = jnp.concatenate(
                [factor_ref[pair_index(w, k, window_count)] for w in range(k + 1, window_count)],
                axis=0,
            )
            after = pl.ds(start + block, width - start - block)
            value = value - (dot(x_parts[0, :, after], factor) + dot(x_parts[1, :, after], factor))
        high, low = split(value)
        x_parts[0, :, pl.ds(start, block)] = high
        x_parts[1, :, pl.ds(start, block)] = low
        window_ref[:, pl.ds(start, block)] = value
    for k in range(window_count - 1, -1, -1):
        start = k * block
        value = window_ref[pl.ds(start, block), :]
        if k + 1 < window_count:
            factor = jnp.concatenate(
                [factor_t[pair_index(w, k, window_count)] for w in range(k + 1, window_count)],
                axis=1,
            )
            after = pl.ds(start + block, width - start - block)
            value = value - (dot(factor, w_parts[0, after, :]) + dot(factor, w_parts[1, after, :]))
            window_ref[pl.ds(start, block), :] = value
        high, low = split(value)
        w_parts[0, pl.ds(start, block), :] = high
        w_parts[1, pl.ds(start, block), :] = low

    for turn in range(local_blocks // 2):
        mine = 2 * turn + core

        @pl.when(me == col * local_blocks + mine)
        def _():
            for step in range(1, n_chip):
                remote(
                    panel_ref, panels.at[mine], panel_send.at[turn, step], panel_recv.at[mine], partner, col
                ).wait_send()

        remote(
            panels.at[mine], panels.at[mine], panel_fwd.at[turn], panel_recv.at[mine], partner, col
        ).wait_send()
    for step in range(1, n_col):
        remote(
            product.at[col], product_in.at[col], product_send.at[step], product_recv.at[col], me, col
        ).wait_send()
        remote(sums.at[col], sums.at[col], sums_send.at[step], sums_recv.at[col], me, col).wait_send()
        remote(
            pieces.at[me, col], pieces.at[me, col], piece_send.at[step], piece_recv.at[col], me, col
        ).wait_send()
    for step in range(1, n_row):
        remote(
            inner.at[me], inner_in.at[me], inner_send.at[step], inner_recv.at[me], partner, col
        ).wait_send()
    for step in range(1, n_chip):
        remote(pieces.at[me], pieces.at[me], row_send.at[step], row_recv.at[me], partner, col).wait_send()
    for source in range(n_chip):
        remote(
            pieces.at[me], pieces.at[me], row_fwd.at[source], row_recv.at[me], partner, col
        ).wait_send()


def solution(mesh):
    n_row, n_col = mesh.shape["prow"], mesh.shape["pcol"]

    def shards(cov_trail, factor_panel, first_level, block_slot, factor_window, diag_inverse):
        window_count, block = diag_inverse.shape[0], diag_inverse.shape[-1]
        rows, cols = cov_trail.shape
        width = window_count * block
        chunk = width // n_col
        piece = width // n_row
        local_blocks = cols // block
        pairs = factor_window.shape[0]
        vmem = pl.BlockSpec(memory_space=pltpu.VMEM)
        hbm = pl.BlockSpec(memory_space=pltpu.MemorySpace.HBM)
        dma = pltpu.SemaphoreType.DMA
        return pl.pallas_call(
            functools.partial(kernel, (n_row, n_col, window_count, block)),
            out_shape=(
                jax.ShapeDtypeStruct((window_count, rows, block), F32),
                jax.ShapeDtypeStruct((width, width), F32),
            ),
            in_specs=[hbm] * 6,
            out_specs=(vmem, vmem),
            scratch_shapes=[
                pltpu.SMEM(first_level.shape, jnp.int32),
                pltpu.SMEM(block_slot.shape, jnp.int32),
                pltpu.VMEM(cov_trail.shape, F32),
                pltpu.VMEM(factor_panel.shape, BF16),
                pltpu.VMEM(factor_window.shape, BF16),
                pltpu.VMEM(diag_inverse.shape, F32),
                dma((6,)),
                pltpu.VMEM((local_blocks, window_count, block, block), BF16),
                pltpu.VMEM((cols, width), BF16),
                pltpu.VMEM((width, rows), BF16),
                pltpu.VMEM((pairs, block, block), BF16),
                pltpu.VMEM((n_col, rows, chunk), F32),
                pltpu.VMEM((n_col, rows, chunk), F32),
                pltpu.VMEM((n_col, rows, chunk), F32),
                pltpu.VMEM((n_row, piece, chunk), F32),
                pltpu.VMEM((n_row, piece, chunk), F32),
                pltpu.VMEM((n_row, n_col, piece, chunk), F32),
                pltpu.VMEM((2, width, width), BF16),
                pltpu.VMEM((2, width, width), BF16),
                dma((local_blocks // 2, n_row // 2)),
                dma((local_blocks // 2,)),
                dma((local_blocks,)),
                dma((n_col,)),
                dma((n_col,)),
                dma((n_col,)),
                dma((n_col,)),
                dma((n_row,)),
                dma((n_row,)),
                dma((n_col,)),
                dma((n_col,)),
                dma((n_row // 2,)),
                dma((n_row // 2,)),
                dma((n_row,)),
            ],
            compiler_params=pltpu.CompilerParams(
                collective_id=0, has_side_effects=True, vmem_limit_bytes=60 * 1024 * 1024
            ),
        )(first_level, block_slot, cov_trail, factor_panel, factor_window, diag_inverse)

    return jax.shard_map(
        shards,
        mesh=mesh,
        in_specs=(P("prow", "pcol"), P(None, "prow", None), P(), P(), P(), P()),
        out_specs=(P(None, "prow", None), P()),
        check_vma=False,
    )
```

```python
import functools

import jax
import jax.numpy as jnp
from jax import lax
from jax.experimental import pallas as pl
from jax.experimental.pallas import tpu as pltpu
from jax.sharding import PartitionSpec as P

MESH = pl.DeviceIdType.MESH
F32 = jnp.float32
BF16 = jnp.bfloat16


def pair_index(upper, lower, window_count):
    return lower * window_count - lower * (lower + 1) // 2 + upper - lower - 1


def split(value):
    high = value.astype(BF16)
    return high, (value - high.astype(F32)).astype(BF16)


def dot(left, right):
    return jnp.dot(left, right, preferred_element_type=F32)


def kernel(
    sizes,
    first_hbm,
    slot_hbm,
    cov_hbm,
    panel_hbm,
    factor_hbm,
    diag_hbm,
    column_ref,
    window_ref,
    first_ref,
    slot_ref,
    cov_ref,
    panel_ref,
    factor_ref,
    diag_ref,
    load_sem,
    panels,
    masked,
    panel_t,
    factor_t,
    product,
    product_in,
    sums,
    inner,
    inner_in,
    pieces,
    x_parts,
    w_parts,
    panel_send,
    panel_fwd,
    panel_recv,
    product_send,
    product_recv,
    sums_send,
    sums_recv,
    inner_send,
    inner_recv,
    piece_send,
    piece_recv,
    row_send,
    row_fwd,
    row_recv,
):
    n_row, n_col, window_count, block = sizes
    local_blocks = cov_ref.shape[1] // block
    n_chip = n_row // 2
    width = window_count * block
    block_count = first_ref.shape[0]
    row_blocks = cov_ref.shape[0] // block
    chunk = product.shape[2]
    piece_rows = width // n_row
    me = lax.axis_index("prow")
    col = lax.axis_index("pcol")
    core = lax.rem(me, 2)
    chip = me // 2
    partner = chip * 2 + 1 - core

    def remote(src, dst, send, recv, row, column):
        return pltpu.make_async_remote_copy(
            src_ref=src,
            dst_ref=dst,
            send_sem=send,
            recv_sem=recv,
            device_id=(row, column),
            device_id_type=MESH,
        )

    def level_of(slot):
        level = jnp.int32(0)
        for index in range(block_count):
            level = level + jnp.where(slot_ref[index] == slot, first_ref[index], 0)
        return level

    loads = [
        pltpu.make_async_copy(source, target, load_sem.at[index])
        for index, (source, target) in enumerate(
            (
                (panel_hbm, panel_ref),
                (first_hbm, first_ref),
                (slot_hbm, slot_ref),
                (cov_hbm, cov_ref),
                (factor_hbm, factor_ref),
                (diag_hbm, diag_ref),
            )
        )
    ]
    for load in loads:
        load.start()
    barrier = pltpu.get_barrier_semaphore()
    for step in range(1, n_row):
        pl.semaphore_signal(
            barrier, inc=1, device_id=(lax.rem(me + step, n_row), col), device_id_type=MESH
        )
    for step in range(1, n_col):
        pl.semaphore_signal(
            barrier, inc=1, device_id=(me, lax.rem(col + step, n_col)), device_id_type=MESH
        )
    pl.semaphore_wait(barrier, n_row + n_col - 2)
    loads[0].wait()

    def panel_copy(src, mine, k, sems, index, row):
        return remote(src.at[k], panels.at[mine, k], sems.at[index], panel_recv.at[mine, k], row, col)

    def other_chips(origin):
        if n_chip == 4:
            side = origin + 1 - 2 * lax.rem(origin, 2)
            return [side, lax.rem(origin + 2, 4)]
        return [lax.rem(origin + step, n_chip) for step in range(1, n_chip)]

    def relay_chip(origin):
        side = origin + 1 - 2 * lax.rem(origin, 2)
        return jnp.where(core == 0, side, lax.rem(origin + 2, 4))

    order = range(window_count)
    for k in order:
        for turn in range(local_blocks // 2):
            mine = 2 * turn + core

            @pl.when(me == col * local_blocks + mine)
            def _():
                for step, target in enumerate(other_chips(chip)):
                    panel_copy(panel_ref, mine, k, panel_send, (turn, k, step), target * 2 + core).start()
                panel_copy(panel_ref, mine, k, panel_fwd, (turn, k), partner).start()
                panels[mine, k] = panel_ref[k]

    loads[1].wait()
    loads[2].wait()
    own_level = level_of(me)
    for k in range(window_count):
        own = jnp.where(own_level <= k, panel_ref[k].astype(F32), 0.0)
        panel_t[pl.ds(k * block, block), :] = own.T.astype(BF16)
    loads[4].wait()
    for index in range(factor_ref.shape[0]):
        factor_t[index] = factor_ref[index].astype(F32).T.astype(BF16)
    loads[3].wait()
    cov_high, cov_low = split(cov_ref[...])
    cov_parts = jnp.concatenate([cov_high, cov_low], axis=0)

    rows = cov_ref.shape[0]
    levels = [level_of(col * local_blocks + index) for index in range(local_blocks)]
    per_block = block // chunk
    for k in order:
        for turn in range(local_blocks // 2):
            mine = 2 * turn + core
            owner = col * local_blocks + mine
            owner_chip = owner // 2

            @pl.when(me != owner)
            def _():
                forward = panel_copy(panels.at[mine], mine, k, panel_fwd, (turn, k), partner)
                forward.wait_recv()
                forward.start()
                if n_chip == 4:

                    @pl.when(chip == relay_chip(owner_chip))
                    def _():
                        panel_copy(
                            panels.at[mine], mine, k, panel_send, (turn, k, 0), (3 - owner_chip) * 2 + core
                        ).start()

        for turn in range(local_blocks // 2):
            other = 2 * turn + 1 - core
            panel_copy(panels.at[other], other, k, panel_fwd, (turn, k), partner).wait_recv()
        for index in range(local_blocks):
            masked[pl.ds(index * block, block), :] = jnp.where(
                levels[index] <= k, panels[index, k].astype(F32), 0.0
            ).astype(BF16)
        both = dot(cov_parts, masked[...])
        partial = both[:rows] + both[rows:]
        for part in range(per_block):
            target = k * per_block + part
            product[target] = partial[:, part * chunk : (part + 1) * chunk]

            @pl.when(col != target)
            def _():
                remote(
                    product.at[target],
                    product_in.at[col],
                    product_send.at[target],
                    product_recv.at[col],
                    me,
                    target,
                ).start()

    total = product[col]
    for step in range(1, n_col):
        source = lax.rem(col + step, n_col)
        remote(
            product.at[source], product_in.at[source], product_send.at[source], product_recv.at[source], me, source
        ).wait_recv()
        total = total + product_in[source]
    sums[col] = total

    def sums_copy(source, way, distance, target):
        return remote(
            sums.at[source], sums.at[source], sums_send.at[way, distance], sums_recv.at[source], me, target
        )

    high, low = split(total)
    inner_both = dot(panel_t[...], jnp.concatenate([high, low], axis=1))
    inner_sum = inner_both[:, :chunk] + inner_both[:, chunk:]
    for index in range(n_row):
        inner[index] = inner_sum[index * piece_rows : (index + 1) * piece_rows]
    for step in range(1, n_row):
        target = lax.rem(me + step, n_row)
        remote(
            inner.at[target], inner_in.at[me], inner_send.at[step], inner_recv.at[me], target, col
        ).start()
    def hop(distance):
        if distance == 0:

            @pl.when(col + 1 < n_col)
            def _():
                sums_copy(col, 0, 0, col + 1).start()

            @pl.when(col > 0)
            def _():
                sums_copy(col, 1, 0, col - 1).start()

            return

        @pl.when(col >= distance)
        def _():
            sums_copy(col - distance, 0, distance, col).wait_recv()

            @pl.when(col + 1 < n_col)
            def _():
                sums_copy(col - distance, 0, distance, col + 1).start()

        @pl.when(col + distance < n_col)
        def _():
            sums_copy(col + distance, 1, distance, col).wait_recv()

            @pl.when(col > 0)
            def _():
                sums_copy(col + distance, 1, distance, col - 1).start()

    hop(0)
    piece = inner[me]
    for step in range(1, n_row):
        source = lax.rem(me + step, n_row)
        remote(
            inner.at[source], inner_in.at[source], inner_send.at[step], inner_recv.at[source], source, col
        ).wait_recv()
        piece = piece + inner_in[source]
    pieces[me, col] = piece
    for step in range(1, n_col):
        target = lax.rem(col + step, n_col)
        remote(
            pieces.at[me, col], pieces.at[me, col], piece_send.at[step], piece_recv.at[col], me, target
        ).start()
    hop(1)
    for step in range(1, n_col):
        source = lax.rem(col + step, n_col)
        remote(
            pieces.at[me, source], pieces.at[me, source], piece_send.at[step], piece_recv.at[source], me, source
        ).wait_recv()
    for step in range(1, n_chip):
        target = lax.rem(chip + step, n_chip) * 2 + core
        remote(
            pieces.at[me], pieces.at[me], row_send.at[step], row_recv.at[me], target, col
        ).start()
    remote(pieces.at[me], pieces.at[me], row_fwd.at[chip], row_recv.at[me], partner, col).start()

    for distance in range(2, n_col):
        hop(distance)
    full = jnp.concatenate([sums[index] for index in range(n_col)], axis=1)
    done_high, done_low = {}, {}
    for k in range(window_count - 1, -1, -1):
        value = full[:, k * block : (k + 1) * block]
        later = range(k + 1, window_count)
        if k + 1 < window_count:
            factor = jnp.concatenate(
                [factor_ref[pair_index(w, k, window_count)] for w in later], axis=0
            )
            left = jnp.concatenate(
                [
                    jnp.concatenate([done_high[w] for w in later], axis=1),
                    jnp.concatenate([done_low[w] for w in later], axis=1),
                ],
                axis=0,
            )
            term = dot(left, factor)
            value = value + (term[:rows] + term[rows:])
        value = -value
        done_high[k], done_low[k] = split(value)
        column_ref[k] = jnp.where(own_level <= k, value, 0.0)

    for step in range(1, n_chip):
        source = lax.rem(chip + step, n_chip)
        row = source * 2 + core
        forward = remote(
            pieces.at[row], pieces.at[row], row_fwd.at[source], row_recv.at[row], partner, col
        )
        forward.wait_recv()
        forward.start()
    for source in range(n_chip):
        row = source * 2 + 1 - core
        remote(
            pieces.at[row], pieces.at[row], row_fwd.at[source], row_recv.at[row], partner, col
        ).wait_recv()

    loads[5].wait()
    known = jnp.concatenate(
        [
            jnp.concatenate([pieces[row, index] for index in range(n_col)], axis=1)
            for row in range(n_row)
        ],
        axis=0,
    )
    for k in range(window_count - 1, -1, -1):
        start = k * block
        value = known[:, start : start + block]
        zero = jnp.zeros((block, block), F32)
        value = value + jnp.concatenate(
            [diag_ref[k] if w == k else zero for w in range(window_count)], axis=0
        )
        if k + 1 < window_count:
            factor = jnp.concatenate(
                [factor_ref[pair_index(w, k, window_count)] for w in range(k + 1, window_count)],
                axis=0,
            )
            after = pl.ds(start + block, width - start - block)
            value = value - (dot(x_parts[0, :, after], factor) + dot(x_parts[1, :, after], factor))
        high, low = split(value)
        x_parts[0, :, pl.ds(start, block)] = high
        x_parts[1, :, pl.ds(start, block)] = low
        window_ref[:, pl.ds(start, block)] = value
    for k in range(window_count - 1, -1, -1):
        start = k * block
        value = window_ref[pl.ds(start, block), :]
        if k + 1 < window_count:
            factor = jnp.concatenate(
                [factor_t[pair_index(w, k, window_count)] for w in range(k + 1, window_count)],
                axis=1,
            )
            after = pl.ds(start + block, width - start - block)
            value = value - (dot(factor, w_parts[0, after, :]) + dot(factor, w_parts[1, after, :]))
            window_ref[pl.ds(start, block), :] = value
        high, low = split(value)
        w_parts[0, pl.ds(start, block), :] = high
        w_parts[1, pl.ds(start, block), :] = low

    for k in order:
        for turn in range(local_blocks // 2):
            mine = 2 * turn + core
            owner = col * local_blocks + mine

            @pl.when(me == owner)
            def _():
                for step, target in enumerate(other_chips(chip)):
                    panel_copy(panel_ref, mine, k, panel_send, (turn, k, step), target * 2 + core).wait_send()

            if n_chip == 4:

                @pl.when((me != owner) & (chip == relay_chip(owner // 2)))
                def _():
                    panel_copy(panel_ref, mine, k, panel_send, (turn, k, 0), partner).wait_send()

            panel_copy(panel_ref, mine, k, panel_fwd, (turn, k), partner).wait_send()
    for target in range(n_col):

        @pl.when(col != target)
        def _():
            remote(
                product.at[target], product_in.at[col], product_send.at[target], product_recv.at[col], me, target
            ).wait_send()

    for distance in range(n_col):

        @pl.when((col >= distance) & (col + 1 < n_col))
        def _():
            sums_copy(col, 0, distance, col + 1).wait_send()

        @pl.when((col + distance < n_col) & (col > 0))
        def _():
            sums_copy(col, 1, distance, col - 1).wait_send()

    for step in range(1, n_col):
        remote(
            pieces.at[me, col], pieces.at[me, col], piece_send.at[step], piece_recv.at[col], me, col
        ).wait_send()
    for step in range(1, n_row):
        remote(
            inner.at[me], inner_in.at[me], inner_send.at[step], inner_recv.at[me], partner, col
        ).wait_send()
    for step in range(1, n_chip):
        remote(pieces.at[me], pieces.at[me], row_send.at[step], row_recv.at[me], partner, col).wait_send()
    for source in range(n_chip):
        remote(
            pieces.at[me], pieces.at[me], row_fwd.at[source], row_recv.at[me], partner, col
        ).wait_send()


def solution(mesh):
    n_row, n_col = mesh.shape["prow"], mesh.shape["pcol"]

    def shards(cov_trail, factor_panel, first_level, block_slot, factor_window, diag_inverse):
        window_count, block = diag_inverse.shape[0], diag_inverse.shape[-1]
        rows, cols = cov_trail.shape
        width = window_count * block
        chunk = width // n_col
        piece = width // n_row
        local_blocks = cols // block
        pairs = factor_window.shape[0]
        vmem = pl.BlockSpec(memory_space=pltpu.VMEM)
        hbm = pl.BlockSpec(memory_space=pltpu.MemorySpace.HBM)
        dma = pltpu.SemaphoreType.DMA
        return pl.pallas_call(
            functools.partial(kernel, (n_row, n_col, window_count, block)),
            out_shape=(
                jax.ShapeDtypeStruct((window_count, rows, block), F32),
                jax.ShapeDtypeStruct((width, width), F32),
            ),
            in_specs=[hbm] * 6,
            out_specs=(vmem, vmem),
            scratch_shapes=[
                pltpu.SMEM(first_level.shape, jnp.int32),
                pltpu.SMEM(block_slot.shape, jnp.int32),
                pltpu.VMEM(cov_trail.shape, F32),
                pltpu.VMEM(factor_panel.shape, BF16),
                pltpu.VMEM(factor_window.shape, BF16),
                pltpu.VMEM(diag_inverse.shape, F32),
                dma((6,)),
                pltpu.VMEM((local_blocks, window_count, block, block), BF16),
                pltpu.VMEM((cols, block), BF16),
                pltpu.VMEM((width, rows), BF16),
                pltpu.VMEM((pairs, block, block), BF16),
                pltpu.VMEM((n_col, rows, chunk), F32),
                pltpu.VMEM((n_col, rows, chunk), F32),
                pltpu.VMEM((n_col, rows, chunk), F32),
                pltpu.VMEM((n_row, piece, chunk), F32),
                pltpu.VMEM((n_row, piece, chunk), F32),
                pltpu.VMEM((n_row, n_col, piece, chunk), F32),
                pltpu.VMEM((2, width, width), BF16),
                pltpu.VMEM((2, width, width), BF16),
                dma((local_blocks // 2, window_count, n_row // 2)),
                dma((local_blocks // 2, window_count)),
                dma((local_blocks, window_count)),
                dma((n_col,)),
                dma((n_col,)),
                dma((2, n_col)),
                dma((n_col,)),
                dma((n_row,)),
                dma((n_row,)),
                dma((n_col,)),
                dma((n_col,)),
                dma((n_row // 2,)),
                dma((n_row // 2,)),
                dma((n_row,)),
            ],
            compiler_params=pltpu.CompilerParams(
                collective_id=0, has_side_effects=True, vmem_limit_bytes=60 * 1024 * 1024
            ),
        )(first_level, block_slot, cov_trail, factor_panel, factor_window, diag_inverse)

    return jax.shard_map(
        shards,
        mesh=mesh,
        in_specs=(P("prow", "pcol"), P(None, "prow", None), P(), P(), P(), P()),
        out_specs=(P(None, "prow", None), P()),
        check_vma=False,
    )
```

```python
import functools

import jax
import jax.numpy as jnp
from jax import lax
from jax.experimental import pallas as pl
from jax.experimental.pallas import tpu as pltpu
from jax.sharding import PartitionSpec as P

MESH = pl.DeviceIdType.MESH
F32 = jnp.float32
BF16 = jnp.bfloat16


def pair_index(upper, lower, window_count):
    return lower * window_count - lower * (lower + 1) // 2 + upper - lower - 1


def split(value):
    high = value.astype(BF16)
    return high, (value - high.astype(F32)).astype(BF16)


def dot(left, right):
    return jnp.dot(left, right, preferred_element_type=F32)


def kernel(
    sizes,
    first_hbm,
    slot_hbm,
    cov_hbm,
    panel_hbm,
    factor_hbm,
    diag_hbm,
    column_ref,
    window_ref,
    first_ref,
    slot_ref,
    cov_ref,
    panel_ref,
    factor_ref,
    diag_ref,
    load_sem,
    panels,
    masked,
    panel_t,
    factor_t,
    product,
    product_in,
    sums,
    inner,
    inner_in,
    pieces,
    x_parts,
    w_parts,
    panel_send,
    panel_fwd,
    panel_recv,
    product_send,
    product_recv,
    sums_send,
    sums_recv,
    inner_send,
    inner_recv,
    piece_send,
    piece_recv,
    row_send,
    row_fwd,
    row_recv,
):
    n_row, n_col, window_count, block = sizes
    local_blocks = cov_ref.shape[1] // block
    n_chip = n_row // 2
    width = window_count * block
    block_count = first_ref.shape[0]
    row_blocks = cov_ref.shape[0] // block
    chunk = product.shape[2]
    piece_rows = pieces.shape[2]
    keep = piece_rows * n_row // block
    me = lax.axis_index("prow")
    col = lax.axis_index("pcol")
    core = lax.rem(me, 2)
    chip = me // 2
    partner = chip * 2 + 1 - core

    def remote(src, dst, send, recv, row, column):
        return pltpu.make_async_remote_copy(
            src_ref=src,
            dst_ref=dst,
            send_sem=send,
            recv_sem=recv,
            device_id=(row, column),
            device_id_type=MESH,
        )

    def level_of(slot):
        level = jnp.int32(0)
        for index in range(block_count):
            level = level + jnp.where(slot_ref[index] == slot, first_ref[index], 0)
        return level

    loads = [
        pltpu.make_async_copy(source, target, load_sem.at[index])
        for index, (source, target) in enumerate(
            (
                (panel_hbm, panel_ref),
                (first_hbm, first_ref),
                (slot_hbm, slot_ref),
                (cov_hbm, cov_ref),
                (factor_hbm, factor_ref),
                (diag_hbm, diag_ref),
            )
        )
    ]
    for load in loads:
        load.start()
    barrier = pltpu.get_barrier_semaphore()
    for step in range(1, n_row):
        pl.semaphore_signal(
            barrier, inc=1, device_id=(lax.rem(me + step, n_row), col), device_id_type=MESH
        )
    for step in range(1, n_col):
        pl.semaphore_signal(
            barrier, inc=1, device_id=(me, lax.rem(col + step, n_col)), device_id_type=MESH
        )
    pl.semaphore_wait(barrier, n_row + n_col - 2)
    loads[0].wait()

    def panel_copy(src, mine, k, sems, index, row):
        return remote(src.at[k], panels.at[mine, k], sems.at[index], panel_recv.at[mine, k], row, col)

    def other_chips(origin):
        if n_chip == 4:
            side = origin + 1 - 2 * lax.rem(origin, 2)
            return [side, lax.rem(origin + 2, 4)]
        return [lax.rem(origin + step, n_chip) for step in range(1, n_chip)]

    def relay_chip(origin):
        side = origin + 1 - 2 * lax.rem(origin, 2)
        return jnp.where(core == 0, side, lax.rem(origin + 2, 4))

    order = range(window_count)
    for k in order:
        for turn in range(local_blocks // 2):
            mine = 2 * turn + core

            @pl.when(me == col * local_blocks + mine)
            def _():
                for step, target in enumerate(other_chips(chip)):
                    panel_copy(panel_ref, mine, k, panel_send, (turn, k, step), target * 2 + core).start()
                panel_copy(panel_ref, mine, k, panel_fwd, (turn, k), partner).start()
                panels[mine, k] = panel_ref[k]

    loads[1].wait()
    loads[2].wait()
    own_level = level_of(me)
    for k in range(window_count):
        own = jnp.where(own_level <= k, panel_ref[k].astype(F32), 0.0)
        panel_t[pl.ds(k * block, block), :] = own.T.astype(BF16)
    loads[4].wait()
    for index in range(factor_ref.shape[0]):
        factor_t[index] = factor_ref[index].astype(F32).T.astype(BF16)
    loads[3].wait()
    cov_high, cov_low = split(cov_ref[...])
    cov_parts = jnp.concatenate([cov_high, cov_low], axis=0)

    rows = cov_ref.shape[0]
    levels = [level_of(col * local_blocks + index) for index in range(local_blocks)]
    per_block = block // chunk
    for k in order:
        for turn in range(local_blocks // 2):
            mine = 2 * turn + core
            owner = col * local_blocks + mine
            owner_chip = owner // 2

            @pl.when(me != owner)
            def _():
                forward = panel_copy(panels.at[mine], mine, k, panel_fwd, (turn, k), partner)
                forward.wait_recv()
                forward.start()
                if n_chip == 4:

                    @pl.when(chip == relay_chip(owner_chip))
                    def _():
                        panel_copy(
                            panels.at[mine], mine, k, panel_send, (turn, k, 0), (3 - owner_chip) * 2 + core
                        ).start()

        for turn in range(local_blocks // 2):
            other = 2 * turn + 1 - core
            panel_copy(panels.at[other], other, k, panel_fwd, (turn, k), partner).wait_recv()
        for index in range(local_blocks):
            masked[pl.ds(index * block, block), :] = jnp.where(
                levels[index] <= k, panels[index, k].astype(F32), 0.0
            ).astype(BF16)
        both = dot(cov_parts, masked[...])
        partial = both[:rows] + both[rows:]
        for part in range(per_block):
            target = k * per_block + part
            product[target] = partial[:, part * chunk : (part + 1) * chunk]

            @pl.when(col != target)
            def _():
                remote(
                    product.at[target],
                    product_in.at[col],
                    product_send.at[target],
                    product_recv.at[col],
                    me,
                    target,
                ).start()

    total = product[col]
    for step in range(1, n_col):
        source = lax.rem(col + step, n_col)
        remote(
            product.at[source], product_in.at[source], product_send.at[source], product_recv.at[source], me, source
        ).wait_recv()
        total = total + product_in[source]
    sums[col] = total

    def sums_copy(source, way, distance, target):
        return remote(
            sums.at[source], sums.at[source], sums_send.at[way, distance], sums_recv.at[source], me, target
        )

    high, low = split(total)
    first = col * window_count // n_col
    kept = jnp.concatenate(
        [
            panel_t[pl.ds(pl.multiple_of(lax.rem(first + t, window_count) * block, block), block), :]
            for t in range(keep)
        ],
        axis=0,
    )
    inner_both = dot(kept, jnp.concatenate([high, low], axis=1))
    inner_sum = inner_both[:, :chunk] + inner_both[:, chunk:]
    for index in range(n_row):
        inner[index] = inner_sum[index * piece_rows : (index + 1) * piece_rows]
    for step in range(1, n_row):
        target = lax.rem(me + step, n_row)
        remote(
            inner.at[target], inner_in.at[me], inner_send.at[step], inner_recv.at[me], target, col
        ).start()
    def send_sums(distance):
        @pl.when(col + distance < n_col)
        def _():
            sums_copy(col, 0, distance, col + distance).start()

        @pl.when(col >= distance)
        def _():
            sums_copy(col, 1, distance, col - distance).start()

    send_sums(1)
    piece = inner[me]
    for step in range(1, n_row):
        source = lax.rem(me + step, n_row)
        remote(
            inner.at[source], inner_in.at[source], inner_send.at[step], inner_recv.at[source], source, col
        ).wait_recv()
        piece = piece + inner_in[source]
    pieces[me, col] = piece
    for step in range(1, n_col):
        target = lax.rem(col + step, n_col)
        remote(
            pieces.at[me, col], pieces.at[me, col], piece_send.at[step], piece_recv.at[col], me, target
        ).start()
    for step in range(1, n_col):
        source = lax.rem(col + step, n_col)
        remote(
            pieces.at[me, source], pieces.at[me, source], piece_send.at[step], piece_recv.at[source], me, source
        ).wait_recv()
    for step in range(1, n_chip):
        target = lax.rem(chip + step, n_chip) * 2 + core
        remote(
            pieces.at[me], pieces.at[me], row_send.at[step], row_recv.at[me], target, col
        ).start()
    remote(pieces.at[me], pieces.at[me], row_fwd.at[chip], row_recv.at[me], partner, col).start()

    for distance in range(2, n_col):
        send_sums(distance)
    for step in range(1, n_chip):
        source = lax.rem(chip + step, n_chip)
        row = source * 2 + core
        forward = remote(
            pieces.at[row], pieces.at[row], row_fwd.at[source], row_recv.at[row], partner, col
        )
        forward.wait_recv()
        forward.start()
    for step in range(1, n_col):
        source = lax.rem(col + step, n_col)
        sums_copy(source, 0, 0, col).wait_recv()
    full = jnp.concatenate([sums[index] for index in range(n_col)], axis=1)
    done_high, done_low = {}, {}
    for k in range(window_count - 1, -1, -1):
        value = full[:, k * block : (k + 1) * block]
        later = range(k + 1, window_count)
        if k + 1 < window_count:
            factor = jnp.concatenate(
                [factor_ref[pair_index(w, k, window_count)] for w in later], axis=0
            )
            left = jnp.concatenate(
                [
                    jnp.concatenate([done_high[w] for w in later], axis=1),
                    jnp.concatenate([done_low[w] for w in later], axis=1),
                ],
                axis=0,
            )
            term = dot(left, factor)
            value = value + (term[:rows] + term[rows:])
        value = -value
        done_high[k], done_low[k] = split(value)
        column_ref[k] = jnp.where(own_level <= k, value, 0.0)

    for source in range(n_chip):
        row = source * 2 + 1 - core
        remote(
            pieces.at[row], pieces.at[row], row_fwd.at[source], row_recv.at[row], partner, col
        ).wait_recv()

    loads[5].wait()
    given = {}
    for k in range(window_count):
        stack = jnp.concatenate(
            [
                jnp.concatenate(
                    [pieces[row, k * per_block + part] for part in range(per_block)], axis=1
                )
                for row in range(n_row)
            ],
            axis=0,
        )
        for t in range(keep):
            given[(k + t) % window_count, k] = stack[t * block : (t + 1) * block]
    for k in range(window_count - 1, -1, -1):
        start = k * block
        value = jnp.concatenate(
            [given[w, k] if (w, k) in given else given[k, w].T for w in range(window_count)], axis=0
        )
        zero = jnp.zeros((block, block), F32)
        value = value + jnp.concatenate(
            [diag_ref[k] if w == k else zero for w in range(window_count)], axis=0
        )
        if k + 1 < window_count:
            factor = jnp.concatenate(
                [factor_ref[pair_index(w, k, window_count)] for w in range(k + 1, window_count)],
                axis=0,
            )
            after = pl.ds(start + block, width - start - block)
            value = value - (dot(x_parts[0, :, after], factor) + dot(x_parts[1, :, after], factor))
        high, low = split(value)
        x_parts[0, :, pl.ds(start, block)] = high
        x_parts[1, :, pl.ds(start, block)] = low
        window_ref[:, pl.ds(start, block)] = value
    for k in range(window_count - 1, -1, -1):
        start = k * block
        value = window_ref[pl.ds(start, block), :]
        if k + 1 < window_count:
            factor = jnp.concatenate(
                [factor_t[pair_index(w, k, window_count)] for w in range(k + 1, window_count)],
                axis=1,
            )
            after = pl.ds(start + block, width - start - block)
            value = value - (dot(factor, w_parts[0, after, :]) + dot(factor, w_parts[1, after, :]))
            window_ref[pl.ds(start, block), :] = value
        high, low = split(value)
        w_parts[0, pl.ds(start, block), :] = high
        w_parts[1, pl.ds(start, block), :] = low

    for k in order:
        for turn in range(local_blocks // 2):
            mine = 2 * turn + core
            owner = col * local_blocks + mine

            @pl.when(me == owner)
            def _():
                for step, target in enumerate(other_chips(chip)):
                    panel_copy(panel_ref, mine, k, panel_send, (turn, k, step), target * 2 + core).wait_send()

            if n_chip == 4:

                @pl.when((me != owner) & (chip == relay_chip(owner // 2)))
                def _():
                    panel_copy(panel_ref, mine, k, panel_send, (turn, k, 0), partner).wait_send()

            panel_copy(panel_ref, mine, k, panel_fwd, (turn, k), partner).wait_send()
    for target in range(n_col):

        @pl.when(col != target)
        def _():
            remote(
                product.at[target], product_in.at[col], product_send.at[target], product_recv.at[col], me, target
            ).wait_send()

    for distance in range(1, n_col):

        @pl.when(col + distance < n_col)
        def _():
            sums_copy(col, 0, distance, col + distance).wait_send()

        @pl.when(col >= distance)
        def _():
            sums_copy(col, 1, distance, col - distance).wait_send()

    for step in range(1, n_col):
        remote(
            pieces.at[me, col], pieces.at[me, col], piece_send.at[step], piece_recv.at[col], me, col
        ).wait_send()
    for step in range(1, n_row):
        remote(
            inner.at[me], inner_in.at[me], inner_send.at[step], inner_recv.at[me], partner, col
        ).wait_send()
    for step in range(1, n_chip):
        remote(pieces.at[me], pieces.at[me], row_send.at[step], row_recv.at[me], partner, col).wait_send()
    for source in range(n_chip):
        remote(
            pieces.at[me], pieces.at[me], row_fwd.at[source], row_recv.at[me], partner, col
        ).wait_send()


def solution(mesh):
    n_row, n_col = mesh.shape["prow"], mesh.shape["pcol"]

    def shards(cov_trail, factor_panel, first_level, block_slot, factor_window, diag_inverse):
        window_count, block = diag_inverse.shape[0], diag_inverse.shape[-1]
        rows, cols = cov_trail.shape
        width = window_count * block
        chunk = width // n_col
        kept = (window_count // 2 + 1) * block
        piece = (kept if kept % (8 * n_row) == 0 else width) // n_row
        local_blocks = cols // block
        pairs = factor_window.shape[0]
        vmem = pl.BlockSpec(memory_space=pltpu.VMEM)
        hbm = pl.BlockSpec(memory_space=pltpu.MemorySpace.HBM)
        dma = pltpu.SemaphoreType.DMA
        return pl.pallas_call(
            functools.partial(kernel, (n_row, n_col, window_count, block)),
            out_shape=(
                jax.ShapeDtypeStruct((window_count, rows, block), F32),
                jax.ShapeDtypeStruct((width, width), F32),
            ),
            in_specs=[hbm] * 6,
            out_specs=(vmem, vmem),
            scratch_shapes=[
                pltpu.SMEM(first_level.shape, jnp.int32),
                pltpu.SMEM(block_slot.shape, jnp.int32),
                pltpu.VMEM(cov_trail.shape, F32),
                pltpu.VMEM(factor_panel.shape, BF16),
                pltpu.VMEM(factor_window.shape, BF16),
                pltpu.VMEM(diag_inverse.shape, F32),
                dma((6,)),
                pltpu.VMEM((local_blocks, window_count, block, block), BF16),
                pltpu.VMEM((cols, block), BF16),
                pltpu.VMEM((width, rows), BF16),
                pltpu.VMEM((pairs, block, block), BF16),
                pltpu.VMEM((n_col, rows, chunk), F32),
                pltpu.VMEM((n_col, rows, chunk), F32),
                pltpu.VMEM((n_col, rows, chunk), F32),
                pltpu.VMEM((n_row, piece, chunk), F32),
                pltpu.VMEM((n_row, piece, chunk), F32),
                pltpu.VMEM((n_row, n_col, piece, chunk), F32),
                pltpu.VMEM((2, width, width), BF16),
                pltpu.VMEM((2, width, width), BF16),
                dma((local_blocks // 2, window_count, n_row // 2)),
                dma((local_blocks // 2, window_count)),
                dma((local_blocks, window_count)),
                dma((n_col,)),
                dma((n_col,)),
                dma((2, n_col)),
                dma((n_col,)),
                dma((n_row,)),
                dma((n_row,)),
                dma((n_col,)),
                dma((n_col,)),
                dma((n_row // 2,)),
                dma((n_row // 2,)),
                dma((n_row,)),
            ],
            compiler_params=pltpu.CompilerParams(
                collective_id=0, has_side_effects=True, vmem_limit_bytes=60 * 1024 * 1024
            ),
        )(first_level, block_slot, cov_trail, factor_panel, factor_window, diag_inverse)

    return jax.shard_map(
        shards,
        mesh=mesh,
        in_specs=(P("prow", "pcol"), P(None, "prow", None), P(), P(), P(), P()),
        out_specs=(P(None, "prow", None), P()),
        check_vma=False,
    )
```

```python
import functools

import jax
import jax.numpy as jnp
from jax import lax
from jax.experimental import pallas as pl
from jax.experimental.pallas import tpu as pltpu
from jax.sharding import PartitionSpec as P

MESH = pl.DeviceIdType.MESH
F32 = jnp.float32
BF16 = jnp.bfloat16


def pair_index(upper, lower, window_count):
    return lower * window_count - lower * (lower + 1) // 2 + upper - lower - 1


def split(value):
    high = value.astype(BF16)
    return high, (value - high.astype(F32)).astype(BF16)


def dot(left, right):
    return jnp.dot(left, right, preferred_element_type=F32)


def kernel(
    sizes,
    first_hbm,
    slot_hbm,
    cov_hbm,
    panel_hbm,
    factor_hbm,
    diag_hbm,
    column_ref,
    window_ref,
    first_ref,
    slot_ref,
    cov_ref,
    panel_ref,
    factor_ref,
    diag_ref,
    load_sem,
    panels,
    masked,
    panel_t,
    factor_t,
    product,
    product_in,
    sums,
    inner,
    inner_in,
    pieces,
    x_parts,
    w_parts,
    panel_send,
    panel_fwd,
    panel_recv,
    product_send,
    product_recv,
    sums_send,
    sums_recv,
    inner_send,
    inner_recv,
    piece_send,
    piece_recv,
    row_send,
    row_fwd,
    row_recv,
):
    n_row, n_col, window_count, block = sizes
    local_blocks = cov_ref.shape[1] // block
    n_chip = n_row // 2
    width = window_count * block
    block_count = first_ref.shape[0]
    row_blocks = cov_ref.shape[0] // block
    chunk = product.shape[2]
    piece_rows = pieces.shape[2]
    keep = piece_rows * n_row // block
    me = lax.axis_index("prow")
    col = lax.axis_index("pcol")
    core = lax.rem(me, 2)
    chip = me // 2
    partner = chip * 2 + 1 - core

    def remote(src, dst, send, recv, row, column):
        return pltpu.make_async_remote_copy(
            src_ref=src,
            dst_ref=dst,
            send_sem=send,
            recv_sem=recv,
            device_id=(row, column),
            device_id_type=MESH,
        )

    def level_of(slot):
        level = jnp.int32(0)
        for index in range(block_count):
            level = level + jnp.where(slot_ref[index] == slot, first_ref[index], 0)
        return level

    loads = [
        pltpu.make_async_copy(source, target, load_sem.at[index])
        for index, (source, target) in enumerate(
            (
                (panel_hbm, panel_ref),
                (first_hbm, first_ref),
                (slot_hbm, slot_ref),
                (cov_hbm, cov_ref),
                (factor_hbm, factor_ref),
                (diag_hbm, diag_ref),
            )
        )
    ]
    for load in loads:
        load.start()
    barrier = pltpu.get_barrier_semaphore()
    for step in range(1, n_row):
        pl.semaphore_signal(
            barrier, inc=1, device_id=(lax.rem(me + step, n_row), col), device_id_type=MESH
        )
    for step in range(1, n_col):
        pl.semaphore_signal(
            barrier, inc=1, device_id=(me, lax.rem(col + step, n_col)), device_id_type=MESH
        )
    pl.semaphore_wait(barrier, n_row + n_col - 2)
    loads[0].wait()

    def panel_copy(src, mine, k, sems, index, row):
        return remote(src.at[k], panels.at[mine, k], sems.at[index], panel_recv.at[mine, k], row, col)

    def other_chips(origin):
        if n_chip == 4:
            side = origin + 1 - 2 * lax.rem(origin, 2)
            return [side, lax.rem(origin + 2, 4)]
        return [lax.rem(origin + step, n_chip) for step in range(1, n_chip)]

    def relay_chip(origin):
        side = origin + 1 - 2 * lax.rem(origin, 2)
        return jnp.where(core == 0, side, lax.rem(origin + 2, 4))

    order = range(window_count)
    for k in order:
        for turn in range(local_blocks // 2):
            mine = 2 * turn + core

            @pl.when(me == col * local_blocks + mine)
            def _():
                for step, target in enumerate(other_chips(chip)):
                    panel_copy(panel_ref, mine, k, panel_send, (turn, k, step), target * 2 + core).start()
                panel_copy(panel_ref, mine, k, panel_fwd, (turn, k), partner).start()
                panels[mine, k] = panel_ref[k]

    loads[1].wait()
    loads[2].wait()
    own_level = level_of(me)
    for k in range(window_count):
        own = jnp.where(own_level <= k, panel_ref[k].astype(F32), 0.0)
        panel_t[pl.ds(k * block, block), :] = own.T.astype(BF16)
    loads[4].wait()
    for index in range(factor_ref.shape[0]):
        factor_t[index] = factor_ref[index].astype(F32).T.astype(BF16)
    loads[3].wait()
    cov_high, cov_low = split(cov_ref[...])
    cov_parts = jnp.concatenate([cov_high, cov_low], axis=0)

    rows = cov_ref.shape[0]
    levels = [level_of(col * local_blocks + index) for index in range(local_blocks)]
    per_block = block // chunk
    for k in order:
        for turn in range(local_blocks // 2):
            mine = 2 * turn + core
            owner = col * local_blocks + mine
            owner_chip = owner // 2

            @pl.when(me != owner)
            def _():
                forward = panel_copy(panels.at[mine], mine, k, panel_fwd, (turn, k), partner)
                forward.wait_recv()
                forward.start()
                if n_chip == 4:

                    @pl.when(chip == relay_chip(owner_chip))
                    def _():
                        panel_copy(
                            panels.at[mine], mine, k, panel_send, (turn, k, 0), (3 - owner_chip) * 2 + core
                        ).start()

        for turn in range(local_blocks // 2):
            other = 2 * turn + 1 - core
            panel_copy(panels.at[other], other, k, panel_fwd, (turn, k), partner).wait_recv()
        for index in range(local_blocks):
            masked[pl.ds(index * block, block), :] = jnp.where(
                levels[index] <= k, panels[index, k].astype(F32), 0.0
            ).astype(BF16)
        both = dot(cov_parts, masked[...])
        partial = both[:rows] + both[rows:]
        for part in range(per_block):
            target = k * per_block + part
            product[target] = partial[:, part * chunk : (part + 1) * chunk]

            @pl.when(col != target)
            def _():
                remote(
                    product.at[target],
                    product_in.at[col],
                    product_send.at[target],
                    product_recv.at[col],
                    me,
                    target,
                ).start()

    total = product[col]
    for step in range(1, n_col):
        source = lax.rem(col + step, n_col)
        remote(
            product.at[source], product_in.at[source], product_send.at[source], product_recv.at[source], me, source
        ).wait_recv()
        total = total + product_in[source]
    sums[col] = total

    def sums_copy(source, way, distance, target):
        return remote(
            sums.at[source], sums.at[source], sums_send.at[way, distance], sums_recv.at[source], me, target
        )

    high, low = split(total)
    first = col * window_count // n_col
    kept = jnp.concatenate(
        [
            panel_t[pl.ds(pl.multiple_of(lax.rem(first + t, window_count) * block, block), block), :]
            for t in range(keep)
        ],
        axis=0,
    )
    inner_both = dot(kept, jnp.concatenate([high, low], axis=1))
    inner_sum = inner_both[:, :chunk] + inner_both[:, chunk:]
    for index in range(n_row):
        inner[index] = inner_sum[index * piece_rows : (index + 1) * piece_rows]
    for step in range(1, n_row):
        target = lax.rem(me + step, n_row)
        remote(
            inner.at[target], inner_in.at[me], inner_send.at[step], inner_recv.at[me], target, col
        ).start()
    def send_sums(distance):
        @pl.when(col + distance < n_col)
        def _():
            sums_copy(col, 0, distance, col + distance).start()

        @pl.when(col >= distance)
        def _():
            sums_copy(col, 1, distance, col - distance).start()

    send_sums(1)
    piece = inner[me]
    for step in range(1, n_row):
        source = lax.rem(me + step, n_row)
        remote(
            inner.at[source], inner_in.at[source], inner_send.at[step], inner_recv.at[source], source, col
        ).wait_recv()
        piece = piece + inner_in[source]
    pieces[me, col] = piece
    for step in range(1, n_col):
        target = lax.rem(col + step, n_col)
        remote(
            pieces.at[me, col], pieces.at[me, col], piece_send.at[step], piece_recv.at[col], me, target
        ).start()
    def row_copy(row, index, sems, slot, target):
        return remote(
            pieces.at[row, index], pieces.at[row, index], sems.at[slot, index], row_recv.at[row, index], target, col
        )

    for turn in range(n_col):
        index = lax.rem(col + turn, n_col)
        if turn:
            remote(
                pieces.at[me, index], pieces.at[me, index], piece_send.at[turn], piece_recv.at[index], me, index
            ).wait_recv()
        for step in range(1, n_chip):
            row_copy(me, index, row_send, step, lax.rem(chip + step, n_chip) * 2 + core).start()
        row_copy(me, index, row_fwd, chip, partner).start()
    for distance in range(2, n_col):
        send_sums(distance)
    for turn in range(n_col):
        index = lax.rem(col + turn, n_col)
        for step in range(1, n_chip):
            source = lax.rem(chip + step, n_chip)
            forward = row_copy(source * 2 + core, index, row_fwd, source, partner)
            forward.wait_recv()
            forward.start()
    for step in range(1, n_col):
        source = lax.rem(col + step, n_col)
        sums_copy(source, 0, 0, col).wait_recv()
    full = jnp.concatenate([sums[index] for index in range(n_col)], axis=1)
    done_high, done_low = {}, {}
    for k in range(window_count - 1, -1, -1):
        value = full[:, k * block : (k + 1) * block]
        later = range(k + 1, window_count)
        if k + 1 < window_count:
            factor = jnp.concatenate(
                [factor_ref[pair_index(w, k, window_count)] for w in later], axis=0
            )
            left = jnp.concatenate(
                [
                    jnp.concatenate([done_high[w] for w in later], axis=1),
                    jnp.concatenate([done_low[w] for w in later], axis=1),
                ],
                axis=0,
            )
            term = dot(left, factor)
            value = value + (term[:rows] + term[rows:])
        value = -value
        done_high[k], done_low[k] = split(value)
        column_ref[k] = jnp.where(own_level <= k, value, 0.0)

    for source in range(n_chip):
        for index in range(n_col):
            row_copy(source * 2 + 1 - core, index, row_fwd, source, partner).wait_recv()

    loads[5].wait()
    given = {}
    for k in range(window_count):
        stack = jnp.concatenate(
            [
                jnp.concatenate(
                    [pieces[row, k * per_block + part] for part in range(per_block)], axis=1
                )
                for row in range(n_row)
            ],
            axis=0,
        )
        for t in range(keep):
            given[(k + t) % window_count, k] = stack[t * block : (t + 1) * block]
    for k in range(window_count - 1, -1, -1):
        start = k * block
        value = jnp.concatenate(
            [given[w, k] if (w, k) in given else given[k, w].T for w in range(window_count)], axis=0
        )
        zero = jnp.zeros((block, block), F32)
        value = value + jnp.concatenate(
            [diag_ref[k] if w == k else zero for w in range(window_count)], axis=0
        )
        if k + 1 < window_count:
            factor = jnp.concatenate(
                [factor_ref[pair_index(w, k, window_count)] for w in range(k + 1, window_count)],
                axis=0,
            )
            after = pl.ds(start + block, width - start - block)
            value = value - (dot(x_parts[0, :, after], factor) + dot(x_parts[1, :, after], factor))
        high, low = split(value)
        x_parts[0, :, pl.ds(start, block)] = high
        x_parts[1, :, pl.ds(start, block)] = low
        window_ref[:, pl.ds(start, block)] = value
    for k in range(window_count - 1, -1, -1):
        start = k * block
        value = window_ref[pl.ds(start, block), :]
        if k + 1 < window_count:
            factor = jnp.concatenate(
                [factor_t[pair_index(w, k, window_count)] for w in range(k + 1, window_count)],
                axis=1,
            )
            after = pl.ds(start + block, width - start - block)
            value = value - (dot(factor, w_parts[0, after, :]) + dot(factor, w_parts[1, after, :]))
            window_ref[pl.ds(start, block), :] = value
        high, low = split(value)
        w_parts[0, pl.ds(start, block), :] = high
        w_parts[1, pl.ds(start, block), :] = low

    for k in order:
        for turn in range(local_blocks // 2):
            mine = 2 * turn + core
            owner = col * local_blocks + mine

            @pl.when(me == owner)
            def _():
                for step, target in enumerate(other_chips(chip)):
                    panel_copy(panel_ref, mine, k, panel_send, (turn, k, step), target * 2 + core).wait_send()

            if n_chip == 4:

                @pl.when((me != owner) & (chip == relay_chip(owner // 2)))
                def _():
                    panel_copy(panel_ref, mine, k, panel_send, (turn, k, 0), partner).wait_send()

            panel_copy(panel_ref, mine, k, panel_fwd, (turn, k), partner).wait_send()
    for target in range(n_col):

        @pl.when(col != target)
        def _():
            remote(
                product.at[target], product_in.at[col], product_send.at[target], product_recv.at[col], me, target
            ).wait_send()

    for distance in range(1, n_col):

        @pl.when(col + distance < n_col)
        def _():
            sums_copy(col, 0, distance, col + distance).wait_send()

        @pl.when(col >= distance)
        def _():
            sums_copy(col, 1, distance, col - distance).wait_send()

    for step in range(1, n_col):
        remote(
            pieces.at[me, col], pieces.at[me, col], piece_send.at[step], piece_recv.at[col], me, col
        ).wait_send()
    for step in range(1, n_row):
        remote(
            inner.at[me], inner_in.at[me], inner_send.at[step], inner_recv.at[me], partner, col
        ).wait_send()
    for index in range(n_col):
        for step in range(1, n_chip):
            row_copy(me, index, row_send, step, partner).wait_send()
        for source in range(n_chip):
            row_copy(me, index, row_fwd, source, partner).wait_send()


def solution(mesh):
    n_row, n_col = mesh.shape["prow"], mesh.shape["pcol"]

    def shards(cov_trail, factor_panel, first_level, block_slot, factor_window, diag_inverse):
        window_count, block = diag_inverse.shape[0], diag_inverse.shape[-1]
        rows, cols = cov_trail.shape
        width = window_count * block
        chunk = width // n_col
        kept = (window_count // 2 + 1) * block
        piece = (kept if kept % (8 * n_row) == 0 else width) // n_row
        local_blocks = cols // block
        pairs = factor_window.shape[0]
        vmem = pl.BlockSpec(memory_space=pltpu.VMEM)
        hbm = pl.BlockSpec(memory_space=pltpu.MemorySpace.HBM)
        dma = pltpu.SemaphoreType.DMA
        return pl.pallas_call(
            functools.partial(kernel, (n_row, n_col, window_count, block)),
            out_shape=(
                jax.ShapeDtypeStruct((window_count, rows, block), F32),
                jax.ShapeDtypeStruct((width, width), F32),
            ),
            in_specs=[hbm] * 6,
            out_specs=(vmem, vmem),
            scratch_shapes=[
                pltpu.SMEM(first_level.shape, jnp.int32),
                pltpu.SMEM(block_slot.shape, jnp.int32),
                pltpu.VMEM(cov_trail.shape, F32),
                pltpu.VMEM(factor_panel.shape, BF16),
                pltpu.VMEM(factor_window.shape, BF16),
                pltpu.VMEM(diag_inverse.shape, F32),
                dma((6,)),
                pltpu.VMEM((local_blocks, window_count, block, block), BF16),
                pltpu.VMEM((cols, block), BF16),
                pltpu.VMEM((width, rows), BF16),
                pltpu.VMEM((pairs, block, block), BF16),
                pltpu.VMEM((n_col, rows, chunk), F32),
                pltpu.VMEM((n_col, rows, chunk), F32),
                pltpu.VMEM((n_col, rows, chunk), F32),
                pltpu.VMEM((n_row, piece, chunk), F32),
                pltpu.VMEM((n_row, piece, chunk), F32),
                pltpu.VMEM((n_row, n_col, piece, chunk), F32),
                pltpu.VMEM((2, width, width), BF16),
                pltpu.VMEM((2, width, width), BF16),
                dma((local_blocks // 2, window_count, n_row // 2)),
                dma((local_blocks // 2, window_count)),
                dma((local_blocks, window_count)),
                dma((n_col,)),
                dma((n_col,)),
                dma((2, n_col)),
                dma((n_col,)),
                dma((n_row,)),
                dma((n_row,)),
                dma((n_col,)),
                dma((n_col,)),
                dma((n_row // 2, n_col)),
                dma((n_row // 2, n_col)),
                dma((n_row, n_col)),
            ],
            compiler_params=pltpu.CompilerParams(
                collective_id=0, has_side_effects=True, vmem_limit_bytes=40 * 1024 * 1024
            ),
        )(
            *(
                pltpu.with_memory_space_constraint(value, pltpu.MemorySpace.HBM)
                for value in (first_level, block_slot, cov_trail, factor_panel, factor_window, diag_inverse)
            )
        )

    return jax.shard_map(
        shards,
        mesh=mesh,
        in_specs=(P("prow", "pcol"), P(None, "prow", None), P(), P(), P(), P()),
        out_specs=(P(None, "prow", None), P()),
        check_vma=False,
    )
```

```python
import functools

import jax
import jax.numpy as jnp
from jax import lax
from jax.experimental import pallas as pl
from jax.experimental.pallas import tpu as pltpu
from jax.sharding import PartitionSpec as P

MESH = pl.DeviceIdType.MESH
F32 = jnp.float32
BF16 = jnp.bfloat16


def pair_index(upper, lower, window_count):
    return lower * window_count - lower * (lower + 1) // 2 + upper - lower - 1


def split(value):
    high = value.astype(BF16)
    return high, (value - high.astype(F32)).astype(BF16)


def dot(left, right):
    return jnp.dot(left, right, preferred_element_type=F32)


def kernel(
    sizes,
    first_hbm,
    slot_hbm,
    cov_hbm,
    panel_hbm,
    factor_hbm,
    diag_hbm,
    column_ref,
    window_ref,
    first_ref,
    slot_ref,
    cov_ref,
    panel_ref,
    factor_ref,
    diag_ref,
    load_sem,
    panels,
    masked,
    panel_t,
    factor_t,
    product,
    product_in,
    sums,
    inner,
    inner_in,
    pieces,
    x_parts,
    w_parts,
    panel_send,
    panel_fwd,
    panel_recv,
    product_send,
    product_recv,
    sums_send,
    sums_recv,
    inner_send,
    inner_recv,
    piece_send,
    piece_recv,
    row_send,
    row_fwd,
    row_recv,
):
    n_row, n_col, window_count, block = sizes
    local_blocks = cov_ref.shape[1] // block
    n_chip = n_row // 2
    width = window_count * block
    block_count = first_ref.shape[0]
    row_blocks = cov_ref.shape[0] // block
    chunk = product.shape[2]
    piece_rows = pieces.shape[2]
    keep = piece_rows * n_row // block
    me = lax.axis_index("prow")
    col = lax.axis_index("pcol")
    core = lax.rem(me, 2)
    chip = me // 2
    partner = chip * 2 + 1 - core

    def remote(src, dst, send, recv, row, column):
        return pltpu.make_async_remote_copy(
            src_ref=src,
            dst_ref=dst,
            send_sem=send,
            recv_sem=recv,
            device_id=(row, column),
            device_id_type=MESH,
        )

    def level_of(slot):
        level = jnp.int32(0)
        for index in range(block_count):
            level = level + jnp.where(slot_ref[index] == slot, first_ref[index], 0)
        return level

    loads = [
        pltpu.make_async_copy(source, target, load_sem.at[index])
        for index, (source, target) in enumerate(
            (
                (panel_hbm, panel_ref),
                (first_hbm, first_ref),
                (slot_hbm, slot_ref),
                (cov_hbm, cov_ref),
                (factor_hbm, factor_ref),
                (diag_hbm, diag_ref),
            )
        )
    ]
    for load in loads:
        load.start()
    barrier = pltpu.get_barrier_semaphore()
    for step in range(1, n_row):
        pl.semaphore_signal(
            barrier, inc=1, device_id=(lax.rem(me + step, n_row), col), device_id_type=MESH
        )
    for step in range(1, n_col):
        pl.semaphore_signal(
            barrier, inc=1, device_id=(me, lax.rem(col + step, n_col)), device_id_type=MESH
        )
    pl.semaphore_wait(barrier, n_row + n_col - 2)
    loads[0].wait()

    def panel_copy(src, mine, k, sems, index, row):
        return remote(src.at[k], panels.at[mine, k], sems.at[index], panel_recv.at[mine, k], row, col)

    def other_chips(origin):
        if n_chip == 4:
            side = origin + 1 - 2 * lax.rem(origin, 2)
            return [side, lax.rem(origin + 2, 4)]
        return [lax.rem(origin + step, n_chip) for step in range(1, n_chip)]

    def relay_chip(origin):
        side = origin + 1 - 2 * lax.rem(origin, 2)
        return jnp.where(core == 0, side, lax.rem(origin + 2, 4))

    order = range(window_count)
    for k in order:
        for turn in range(local_blocks // 2):
            mine = 2 * turn + core

            @pl.when(me == col * local_blocks + mine)
            def _():
                for step, target in enumerate(other_chips(chip)):
                    panel_copy(panel_ref, mine, k, panel_send, (turn, k, step), target * 2 + core).start()
                panel_copy(panel_ref, mine, k, panel_fwd, (turn, k), partner).start()
                panels[mine, k] = panel_ref[k]

    loads[1].wait()
    loads[2].wait()
    own_level = level_of(me)
    for k in range(window_count):
        own = jnp.where(own_level <= k, panel_ref[k].astype(F32), 0.0)
        panel_t[pl.ds(k * block, block), :] = own.T.astype(BF16)
    loads[4].wait()
    for index in range(factor_ref.shape[0]):
        factor_t[index] = factor_ref[index].astype(F32).T.astype(BF16)
    loads[3].wait()
    cov_high, cov_low = split(cov_ref[...])
    cov_parts = jnp.concatenate([cov_high, cov_low], axis=0)

    rows = cov_ref.shape[0]
    levels = [level_of(col * local_blocks + index) for index in range(local_blocks)]
    per_block = block // chunk
    def arrive(k):
        for turn in range(local_blocks // 2):
            mine = 2 * turn + core
            owner = col * local_blocks + mine
            owner_chip = owner // 2

            @pl.when(me != owner)
            def _():
                forward = panel_copy(panels.at[mine], mine, k, panel_fwd, (turn, k), partner)
                forward.wait_recv()
                forward.start()
                if n_chip == 4:

                    @pl.when(chip == relay_chip(owner_chip))
                    def _():
                        panel_copy(
                            panels.at[mine], mine, k, panel_send, (turn, k, 0), (3 - owner_chip) * 2 + core
                        ).start()

    def multiply(k):
        for turn in range(local_blocks // 2):
            other = 2 * turn + 1 - core
            panel_copy(panels.at[other], other, k, panel_fwd, (turn, k), partner).wait_recv()
        for index in range(local_blocks):
            masked[pl.ds(index * block, block), :] = jnp.where(
                levels[index] <= k, panels[index, k].astype(F32), 0.0
            ).astype(BF16)
        both = dot(cov_parts, masked[...])
        partial = both[:rows] + both[rows:]
        for part in range(per_block):
            target = k * per_block + part
            product[target] = partial[:, part * chunk : (part + 1) * chunk]

            @pl.when(col != target)
            def _():
                remote(
                    product.at[target],
                    product_in.at[col],
                    product_send.at[target],
                    product_recv.at[col],
                    me,
                    target,
                ).start()

    arrive(0)
    for k in order:
        if k + 1 < window_count:
            arrive(k + 1)
        multiply(k)

    total = product[col]
    for step in range(1, n_col):
        source = lax.rem(col + step, n_col)
        remote(
            product.at[source], product_in.at[source], product_send.at[source], product_recv.at[source], me, source
        ).wait_recv()
        total = total + product_in[source]
    sums[col] = total

    def sums_copy(source, way, distance, target):
        return remote(
            sums.at[source], sums.at[source], sums_send.at[way, distance], sums_recv.at[source], me, target
        )

    high, low = split(total)
    first = col * window_count // n_col
    kept = jnp.concatenate(
        [
            panel_t[pl.ds(pl.multiple_of(lax.rem(first + t, window_count) * block, block), block), :]
            for t in range(keep)
        ],
        axis=0,
    )
    inner_both = dot(kept, jnp.concatenate([high, low], axis=1))
    inner_sum = inner_both[:, :chunk] + inner_both[:, chunk:]
    for index in range(n_row):
        inner[index] = inner_sum[index * piece_rows : (index + 1) * piece_rows]
    for step in range(1, n_row):
        target = lax.rem(me + step, n_row)
        remote(
            inner.at[target], inner_in.at[me], inner_send.at[step], inner_recv.at[me], target, col
        ).start()
    def send_sums(distance):
        @pl.when(col + distance < n_col)
        def _():
            sums_copy(col, 0, distance, col + distance).start()

        @pl.when(col >= distance)
        def _():
            sums_copy(col, 1, distance, col - distance).start()

    send_sums(1)
    piece = inner[me]
    for step in range(1, n_row):
        source = lax.rem(me + step, n_row)
        remote(
            inner.at[source], inner_in.at[source], inner_send.at[step], inner_recv.at[source], source, col
        ).wait_recv()
        piece = piece + inner_in[source]
    pieces[me, col] = piece
    for step in range(1, n_col):
        target = lax.rem(col + step, n_col)
        remote(
            pieces.at[me, col], pieces.at[me, col], piece_send.at[step], piece_recv.at[col], me, target
        ).start()
    def row_copy(row, index, sems, slot, target):
        return remote(
            pieces.at[row, index], pieces.at[row, index], sems.at[slot, index], row_recv.at[row, index], target, col
        )

    for turn in range(n_col):
        index = lax.rem(col + turn, n_col)
        if turn:
            remote(
                pieces.at[me, index], pieces.at[me, index], piece_send.at[turn], piece_recv.at[index], me, index
            ).wait_recv()
        for step in range(1, n_chip):
            row_copy(me, index, row_send, step, lax.rem(chip + step, n_chip) * 2 + core).start()
        row_copy(me, index, row_fwd, chip, partner).start()
    for distance in range(2, n_col):
        send_sums(distance)
    for turn in range(n_col):
        index = lax.rem(col + turn, n_col)
        for step in range(1, n_chip):
            source = lax.rem(chip + step, n_chip)
            forward = row_copy(source * 2 + core, index, row_fwd, source, partner)
            forward.wait_recv()
            forward.start()
    for step in range(1, n_col):
        source = lax.rem(col + step, n_col)
        sums_copy(source, 0, 0, col).wait_recv()
    full = jnp.concatenate([sums[index] for index in range(n_col)], axis=1)
    done_high, done_low = {}, {}
    for k in range(window_count - 1, -1, -1):
        value = full[:, k * block : (k + 1) * block]
        later = range(k + 1, window_count)
        if k + 1 < window_count:
            factor = jnp.concatenate(
                [factor_ref[pair_index(w, k, window_count)] for w in later], axis=0
            )
            left = jnp.concatenate(
                [
                    jnp.concatenate([done_high[w] for w in later], axis=1),
                    jnp.concatenate([done_low[w] for w in later], axis=1),
                ],
                axis=0,
            )
            term = dot(left, factor)
            value = value + (term[:rows] + term[rows:])
        value = -value
        done_high[k], done_low[k] = split(value)
        column_ref[k] = jnp.where(own_level <= k, value, 0.0)

    for source in range(n_chip):
        for index in range(n_col):
            row_copy(source * 2 + 1 - core, index, row_fwd, source, partner).wait_recv()

    loads[5].wait()
    given = {}
    for k in range(window_count):
        stack = jnp.concatenate(
            [
                jnp.concatenate(
                    [pieces[row, k * per_block + part] for part in range(per_block)], axis=1
                )
                for row in range(n_row)
            ],
            axis=0,
        )
        for t in range(keep):
            given[(k + t) % window_count, k] = stack[t * block : (t + 1) * block]
    for k in range(window_count - 1, -1, -1):
        start = k * block
        value = jnp.concatenate(
            [given[w, k] if (w, k) in given else given[k, w].T for w in range(window_count)], axis=0
        )
        zero = jnp.zeros((block, block), F32)
        value = value + jnp.concatenate(
            [diag_ref[k] if w == k else zero for w in range(window_count)], axis=0
        )
        if k + 1 < window_count:
            factor = jnp.concatenate(
                [factor_ref[pair_index(w, k, window_count)] for w in range(k + 1, window_count)],
                axis=0,
            )
            after = pl.ds(start + block, width - start - block)
            value = value - (dot(x_parts[0, :, after], factor) + dot(x_parts[1, :, after], factor))
        high, low = split(value)
        x_parts[0, :, pl.ds(start, block)] = high
        x_parts[1, :, pl.ds(start, block)] = low
        window_ref[:, pl.ds(start, block)] = value
    for k in range(window_count - 1, -1, -1):
        start = k * block
        value = window_ref[pl.ds(start, block), :]
        if k + 1 < window_count:
            factor = jnp.concatenate(
                [factor_t[pair_index(w, k, window_count)] for w in range(k + 1, window_count)],
                axis=1,
            )
            after = pl.ds(start + block, width - start - block)
            value = value - (dot(factor, w_parts[0, after, :]) + dot(factor, w_parts[1, after, :]))
            window_ref[pl.ds(start, block), :] = value
        high, low = split(value)
        w_parts[0, pl.ds(start, block), :] = high
        w_parts[1, pl.ds(start, block), :] = low

    for k in order:
        for turn in range(local_blocks // 2):
            mine = 2 * turn + core
            owner = col * local_blocks + mine

            @pl.when(me == owner)
            def _():
                for step, target in enumerate(other_chips(chip)):
                    panel_copy(panel_ref, mine, k, panel_send, (turn, k, step), target * 2 + core).wait_send()

            if n_chip == 4:

                @pl.when((me != owner) & (chip == relay_chip(owner // 2)))
                def _():
                    panel_copy(panel_ref, mine, k, panel_send, (turn, k, 0), partner).wait_send()

            panel_copy(panel_ref, mine, k, panel_fwd, (turn, k), partner).wait_send()
    for target in range(n_col):

        @pl.when(col != target)
        def _():
            remote(
                product.at[target], product_in.at[col], product_send.at[target], product_recv.at[col], me, target
            ).wait_send()

    for distance in range(1, n_col):

        @pl.when(col + distance < n_col)
        def _():
            sums_copy(col, 0, distance, col + distance).wait_send()

        @pl.when(col >= distance)
        def _():
            sums_copy(col, 1, distance, col - distance).wait_send()

    for step in range(1, n_col):
        remote(
            pieces.at[me, col], pieces.at[me, col], piece_send.at[step], piece_recv.at[col], me, col
        ).wait_send()
    for step in range(1, n_row):
        remote(
            inner.at[me], inner_in.at[me], inner_send.at[step], inner_recv.at[me], partner, col
        ).wait_send()
    for index in range(n_col):
        for step in range(1, n_chip):
            row_copy(me, index, row_send, step, partner).wait_send()
        for source in range(n_chip):
            row_copy(me, index, row_fwd, source, partner).wait_send()


def solution(mesh):
    n_row, n_col = mesh.shape["prow"], mesh.shape["pcol"]

    def shards(cov_trail, factor_panel, first_level, block_slot, factor_window, diag_inverse):
        window_count, block = diag_inverse.shape[0], diag_inverse.shape[-1]
        rows, cols = cov_trail.shape
        width = window_count * block
        chunk = width // n_col
        kept = (window_count // 2 + 1) * block
        piece = (kept if kept % (8 * n_row) == 0 else width) // n_row
        local_blocks = cols // block
        pairs = factor_window.shape[0]
        vmem = pl.BlockSpec(memory_space=pltpu.VMEM)
        hbm = pl.BlockSpec(memory_space=pltpu.MemorySpace.HBM)
        dma = pltpu.SemaphoreType.DMA
        return pl.pallas_call(
            functools.partial(kernel, (n_row, n_col, window_count, block)),
            out_shape=(
                jax.ShapeDtypeStruct((window_count, rows, block), F32),
                jax.ShapeDtypeStruct((width, width), F32),
            ),
            in_specs=[hbm] * 6,
            out_specs=(vmem, vmem),
            scratch_shapes=[
                pltpu.SMEM(first_level.shape, jnp.int32),
                pltpu.SMEM(block_slot.shape, jnp.int32),
                pltpu.VMEM(cov_trail.shape, F32),
                pltpu.VMEM(factor_panel.shape, BF16),
                pltpu.VMEM(factor_window.shape, BF16),
                pltpu.VMEM(diag_inverse.shape, F32),
                dma((6,)),
                pltpu.VMEM((local_blocks, window_count, block, block), BF16),
                pltpu.VMEM((cols, block), BF16),
                pltpu.VMEM((width, rows), BF16),
                pltpu.VMEM((pairs, block, block), BF16),
                pltpu.VMEM((n_col, rows, chunk), F32),
                pltpu.VMEM((n_col, rows, chunk), F32),
                pltpu.VMEM((n_col, rows, chunk), F32),
                pltpu.VMEM((n_row, piece, chunk), F32),
                pltpu.VMEM((n_row, piece, chunk), F32),
                pltpu.VMEM((n_row, n_col, piece, chunk), F32),
                pltpu.VMEM((2, width, width), BF16),
                pltpu.VMEM((2, width, width), BF16),
                dma((local_blocks // 2, window_count, n_row // 2)),
                dma((local_blocks // 2, window_count)),
                dma((local_blocks, window_count)),
                dma((n_col,)),
                dma((n_col,)),
                dma((2, n_col)),
                dma((n_col,)),
                dma((n_row,)),
                dma((n_row,)),
                dma((n_col,)),
                dma((n_col,)),
                dma((n_row // 2, n_col)),
                dma((n_row // 2, n_col)),
                dma((n_row, n_col)),
            ],
            compiler_params=pltpu.CompilerParams(
                collective_id=0, has_side_effects=True, vmem_limit_bytes=40 * 1024 * 1024
            ),
        )(
            *(
                pltpu.with_memory_space_constraint(value, pltpu.MemorySpace.HBM)
                for value in (first_level, block_slot, cov_trail, factor_panel, factor_window, diag_inverse)
            )
        )

    return jax.shard_map(
        shards,
        mesh=mesh,
        in_specs=(P("prow", "pcol"), P(None, "prow", None), P(), P(), P(), P()),
        out_specs=(P(None, "prow", None), P()),
        check_vma=False,
    )
```

```python
import functools

import jax
import jax.numpy as jnp
from jax import lax
from jax.experimental import pallas as pl
from jax.experimental.pallas import tpu as pltpu
from jax.sharding import PartitionSpec as P

MESH = pl.DeviceIdType.MESH
F32 = jnp.float32
BF16 = jnp.bfloat16


def pair_index(upper, lower, window_count):
    return lower * window_count - lower * (lower + 1) // 2 + upper - lower - 1


def split(value):
    high = value.astype(BF16)
    return high, (value - high.astype(F32)).astype(BF16)


def dot(left, right):
    return jnp.dot(left, right, preferred_element_type=F32)


def kernel(
    sizes,
    first_hbm,
    slot_hbm,
    cov_hbm,
    panel_hbm,
    factor_hbm,
    diag_hbm,
    column_ref,
    window_ref,
    first_ref,
    slot_ref,
    cov_ref,
    panel_ref,
    factor_ref,
    diag_ref,
    load_sem,
    panels,
    masked,
    panel_t,
    factor_t,
    product,
    product_in,
    sums,
    inner,
    inner_in,
    pieces,
    x_parts,
    w_parts,
    panel_send,
    panel_fwd,
    panel_recv,
    product_send,
    product_recv,
    sums_send,
    sums_recv,
    inner_send,
    inner_recv,
    piece_send,
    piece_recv,
    row_send,
    row_fwd,
    row_recv,
):
    n_row, n_col, window_count, block = sizes
    local_blocks = cov_ref.shape[1] // block
    n_chip = n_row // 2
    width = window_count * block
    block_count = first_ref.shape[0]
    row_blocks = cov_ref.shape[0] // block
    chunk = product.shape[2]
    piece_rows = pieces.shape[2]
    keep = piece_rows * n_row // block
    me = lax.axis_index("prow")
    col = lax.axis_index("pcol")
    core = lax.rem(me, 2)
    chip = me // 2
    partner = chip * 2 + 1 - core

    def remote(src, dst, send, recv, row, column):
        return pltpu.make_async_remote_copy(
            src_ref=src,
            dst_ref=dst,
            send_sem=send,
            recv_sem=recv,
            device_id=(row, column),
            device_id_type=MESH,
        )

    def level_of(slot):
        level = jnp.int32(0)
        for index in range(block_count):
            level = level + jnp.where(slot_ref[index] == slot, first_ref[index], 0)
        return level

    loads = [
        pltpu.make_async_copy(source, target, load_sem.at[index])
        for index, (source, target) in enumerate(
            (
                (panel_hbm, panel_ref),
                (first_hbm, first_ref),
                (slot_hbm, slot_ref),
                (cov_hbm, cov_ref),
                (factor_hbm, factor_ref),
                (diag_hbm, diag_ref),
            )
        )
    ]
    for load in loads:
        load.start()
    barrier = pltpu.get_barrier_semaphore()
    for step in range(1, n_row):
        pl.semaphore_signal(
            barrier, inc=1, device_id=(lax.rem(me + step, n_row), col), device_id_type=MESH
        )
    for step in range(1, n_col):
        pl.semaphore_signal(
            barrier, inc=1, device_id=(me, lax.rem(col + step, n_col)), device_id_type=MESH
        )
    pl.semaphore_wait(barrier, n_row + n_col - 2)
    loads[0].wait()

    def panel_copy(src, mine, k, sems, index, row):
        return remote(src.at[k], panels.at[mine, k], sems.at[index], panel_recv.at[mine, k], row, col)

    def other_chips(origin):
        return [lax.rem(origin + step, n_chip) for step in range(1, n_chip)]

    order = range(window_count)
    for k in order:
        for turn in range(local_blocks // 2):
            mine = 2 * turn + core

            @pl.when(me == col * local_blocks + mine)
            def _():
                for step, target in enumerate(other_chips(chip)):
                    panel_copy(panel_ref, mine, k, panel_send, (turn, k, step), target * 2 + core).start()
                panel_copy(panel_ref, mine, k, panel_fwd, (turn, k), partner).start()
                panels[mine, k] = panel_ref[k]

    loads[1].wait()
    loads[2].wait()
    own_level = level_of(me)
    for k in range(window_count):
        own = jnp.where(own_level <= k, panel_ref[k].astype(F32), 0.0)
        panel_t[pl.ds(k * block, block), :] = own.T.astype(BF16)
    loads[4].wait()
    for index in range(factor_ref.shape[0]):
        factor_t[index] = factor_ref[index].astype(F32).T.astype(BF16)
    loads[3].wait()
    cov_high, cov_low = split(cov_ref[...])
    cov_parts = jnp.concatenate([cov_high, cov_low], axis=0)

    rows = cov_ref.shape[0]
    levels = [level_of(col * local_blocks + index) for index in range(local_blocks)]
    per_block = block // chunk
    def arrive(k):
        for turn in range(local_blocks // 2):
            mine = 2 * turn + core
            owner = col * local_blocks + mine

            @pl.when(me != owner)
            def _():
                forward = panel_copy(panels.at[mine], mine, k, panel_fwd, (turn, k), partner)
                forward.wait_recv()
                forward.start()

    def multiply(k):
        for turn in range(local_blocks // 2):
            other = 2 * turn + 1 - core
            panel_copy(panels.at[other], other, k, panel_fwd, (turn, k), partner).wait_recv()
        for index in range(local_blocks):
            masked[pl.ds(index * block, block), :] = jnp.where(
                levels[index] <= k, panels[index, k].astype(F32), 0.0
            ).astype(BF16)
        both = dot(cov_parts, masked[...])
        partial = both[:rows] + both[rows:]
        for part in range(per_block):
            target = k * per_block + part
            product[target] = partial[:, part * chunk : (part + 1) * chunk]

            @pl.when(col != target)
            def _():
                remote(
                    product.at[target],
                    product_in.at[col],
                    product_send.at[target],
                    product_recv.at[col],
                    me,
                    target,
                ).start()

    arrive(0)
    for k in order:
        if k + 1 < window_count:
            arrive(k + 1)
        multiply(k)

    total = product[col]
    for step in range(1, n_col):
        source = lax.rem(col + step, n_col)
        remote(
            product.at[source], product_in.at[source], product_send.at[source], product_recv.at[source], me, source
        ).wait_recv()
        total = total + product_in[source]
    sums[col] = total

    def sums_copy(source, way, distance, target):
        return remote(
            sums.at[source], sums.at[source], sums_send.at[way, distance], sums_recv.at[source], me, target
        )

    high, low = split(total)
    first = col * window_count // n_col
    kept = jnp.concatenate(
        [
            panel_t[pl.ds(pl.multiple_of(lax.rem(first + t, window_count) * block, block), block), :]
            for t in range(keep)
        ],
        axis=0,
    )
    inner_both = dot(kept, jnp.concatenate([high, low], axis=1))
    inner_sum = inner_both[:, :chunk] + inner_both[:, chunk:]
    for index in range(n_row):
        inner[index] = inner_sum[index * piece_rows : (index + 1) * piece_rows]
    for step in range(1, n_row):
        target = lax.rem(me + step, n_row)
        remote(
            inner.at[target], inner_in.at[me], inner_send.at[step], inner_recv.at[me], target, col
        ).start()
    def send_sums(distance):
        @pl.when(col + distance < n_col)
        def _():
            sums_copy(col, 0, distance, col + distance).start()

        @pl.when(col >= distance)
        def _():
            sums_copy(col, 1, distance, col - distance).start()

    send_sums(1)
    piece = inner[me]
    for step in range(1, n_row):
        source = lax.rem(me + step, n_row)
        remote(
            inner.at[source], inner_in.at[source], inner_send.at[step], inner_recv.at[source], source, col
        ).wait_recv()
        piece = piece + inner_in[source]
    pieces[me, col] = piece
    for step in range(1, n_col):
        target = lax.rem(col + step, n_col)
        remote(
            pieces.at[me, col], pieces.at[me, col], piece_send.at[step], piece_recv.at[col], me, target
        ).start()
    def row_copy(row, index, sems, slot, target):
        return remote(
            pieces.at[row, index], pieces.at[row, index], sems.at[slot, index], row_recv.at[row, index], target, col
        )

    for turn in range(n_col):
        index = lax.rem(col + turn, n_col)
        if turn:
            remote(
                pieces.at[me, index], pieces.at[me, index], piece_send.at[turn], piece_recv.at[index], me, index
            ).wait_recv()
        for step in range(1, n_chip):
            row_copy(me, index, row_send, step, lax.rem(chip + step, n_chip) * 2 + core).start()
        row_copy(me, index, row_fwd, chip, partner).start()
    for distance in range(2, n_col):
        send_sums(distance)
    for turn in range(n_col):
        index = lax.rem(col + turn, n_col)
        for step in range(1, n_chip):
            source = lax.rem(chip + step, n_chip)
            forward = row_copy(source * 2 + core, index, row_fwd, source, partner)
            forward.wait_recv()
            forward.start()
    for step in range(1, n_col):
        source = lax.rem(col + step, n_col)
        sums_copy(source, 0, 0, col).wait_recv()
    full = jnp.concatenate([sums[index] for index in range(n_col)], axis=1)
    done_high, done_low = {}, {}
    for k in range(window_count - 1, -1, -1):
        value = full[:, k * block : (k + 1) * block]
        later = range(k + 1, window_count)
        if k + 1 < window_count:
            factor = jnp.concatenate(
                [factor_ref[pair_index(w, k, window_count)] for w in later], axis=0
            )
            left = jnp.concatenate(
                [
                    jnp.concatenate([done_high[w] for w in later], axis=1),
                    jnp.concatenate([done_low[w] for w in later], axis=1),
                ],
                axis=0,
            )
            term = dot(left, factor)
            value = value + (term[:rows] + term[rows:])
        value = -value
        done_high[k], done_low[k] = split(value)
        column_ref[k] = jnp.where(own_level <= k, value, 0.0)

    for source in range(n_chip):
        for index in range(n_col):
            row_copy(source * 2 + 1 - core, index, row_fwd, source, partner).wait_recv()

    loads[5].wait()
    given = {}
    for k in range(window_count):
        stack = jnp.concatenate(
            [
                jnp.concatenate(
                    [pieces[row, k * per_block + part] for part in range(per_block)], axis=1
                )
                for row in range(n_row)
            ],
            axis=0,
        )
        for t in range(keep):
            given[(k + t) % window_count, k] = stack[t * block : (t + 1) * block]
    for k in range(window_count - 1, -1, -1):
        start = k * block
        value = jnp.concatenate(
            [given[w, k] if (w, k) in given else given[k, w].T for w in range(window_count)], axis=0
        )
        zero = jnp.zeros((block, block), F32)
        value = value + jnp.concatenate(
            [diag_ref[k] if w == k else zero for w in range(window_count)], axis=0
        )
        if k + 1 < window_count:
            factor = jnp.concatenate(
                [factor_ref[pair_index(w, k, window_count)] for w in range(k + 1, window_count)],
                axis=0,
            )
            after = pl.ds(start + block, width - start - block)
            value = value - (dot(x_parts[0, :, after], factor) + dot(x_parts[1, :, after], factor))
        high, low = split(value)
        x_parts[0, :, pl.ds(start, block)] = high
        x_parts[1, :, pl.ds(start, block)] = low
        window_ref[:, pl.ds(start, block)] = value
    for k in range(window_count - 1, -1, -1):
        start = k * block
        value = window_ref[pl.ds(start, block), :]
        if k + 1 < window_count:
            factor = jnp.concatenate(
                [factor_t[pair_index(w, k, window_count)] for w in range(k + 1, window_count)],
                axis=1,
            )
            after = pl.ds(start + block, width - start - block)
            value = value - (dot(factor, w_parts[0, after, :]) + dot(factor, w_parts[1, after, :]))
            window_ref[pl.ds(start, block), :] = value
        high, low = split(value)
        w_parts[0, pl.ds(start, block), :] = high
        w_parts[1, pl.ds(start, block), :] = low

    for k in order:
        for turn in range(local_blocks // 2):
            mine = 2 * turn + core
            owner = col * local_blocks + mine

            @pl.when(me == owner)
            def _():
                for step, target in enumerate(other_chips(chip)):
                    panel_copy(panel_ref, mine, k, panel_send, (turn, k, step), target * 2 + core).wait_send()

            panel_copy(panel_ref, mine, k, panel_fwd, (turn, k), partner).wait_send()
    for target in range(n_col):

        @pl.when(col != target)
        def _():
            remote(
                product.at[target], product_in.at[col], product_send.at[target], product_recv.at[col], me, target
            ).wait_send()

    for distance in range(1, n_col):

        @pl.when(col + distance < n_col)
        def _():
            sums_copy(col, 0, distance, col + distance).wait_send()

        @pl.when(col >= distance)
        def _():
            sums_copy(col, 1, distance, col - distance).wait_send()

    for step in range(1, n_col):
        remote(
            pieces.at[me, col], pieces.at[me, col], piece_send.at[step], piece_recv.at[col], me, col
        ).wait_send()
    for step in range(1, n_row):
        remote(
            inner.at[me], inner_in.at[me], inner_send.at[step], inner_recv.at[me], partner, col
        ).wait_send()
    for index in range(n_col):
        for step in range(1, n_chip):
            row_copy(me, index, row_send, step, partner).wait_send()
        for source in range(n_chip):
            row_copy(me, index, row_fwd, source, partner).wait_send()


def solution(mesh):
    n_row, n_col = mesh.shape["prow"], mesh.shape["pcol"]

    def shards(cov_trail, factor_panel, first_level, block_slot, factor_window, diag_inverse):
        window_count, block = diag_inverse.shape[0], diag_inverse.shape[-1]
        rows, cols = cov_trail.shape
        width = window_count * block
        chunk = width // n_col
        kept = (window_count // 2 + 1) * block
        piece = (kept if kept % (8 * n_row) == 0 else width) // n_row
        local_blocks = cols // block
        pairs = factor_window.shape[0]
        vmem = pl.BlockSpec(memory_space=pltpu.VMEM)
        hbm = pl.BlockSpec(memory_space=pltpu.MemorySpace.HBM)
        dma = pltpu.SemaphoreType.DMA
        return pl.pallas_call(
            functools.partial(kernel, (n_row, n_col, window_count, block)),
            out_shape=(
                jax.ShapeDtypeStruct((window_count, rows, block), F32),
                jax.ShapeDtypeStruct((width, width), F32),
            ),
            in_specs=[hbm] * 6,
            out_specs=(vmem, vmem),
            scratch_shapes=[
                pltpu.SMEM(first_level.shape, jnp.int32),
                pltpu.SMEM(block_slot.shape, jnp.int32),
                pltpu.VMEM(cov_trail.shape, F32),
                pltpu.VMEM(factor_panel.shape, BF16),
                pltpu.VMEM(factor_window.shape, BF16),
                pltpu.VMEM(diag_inverse.shape, F32),
                dma((6,)),
                pltpu.VMEM((local_blocks, window_count, block, block), BF16),
                pltpu.VMEM((cols, block), BF16),
                pltpu.VMEM((width, rows), BF16),
                pltpu.VMEM((pairs, block, block), BF16),
                pltpu.VMEM((n_col, rows, chunk), F32),
                pltpu.VMEM((n_col, rows, chunk), F32),
                pltpu.VMEM((n_col, rows, chunk), F32),
                pltpu.VMEM((n_row, piece, chunk), F32),
                pltpu.VMEM((n_row, piece, chunk), F32),
                pltpu.VMEM((n_row, n_col, piece, chunk), F32),
                pltpu.VMEM((2, width, width), BF16),
                pltpu.VMEM((2, width, width), BF16),
                dma((local_blocks // 2, window_count, n_row // 2)),
                dma((local_blocks // 2, window_count)),
                dma((local_blocks, window_count)),
                dma((n_col,)),
                dma((n_col,)),
                dma((2, n_col)),
                dma((n_col,)),
                dma((n_row,)),
                dma((n_row,)),
                dma((n_col,)),
                dma((n_col,)),
                dma((n_row // 2, n_col)),
                dma((n_row // 2, n_col)),
                dma((n_row, n_col)),
            ],
            compiler_params=pltpu.CompilerParams(
                collective_id=0, has_side_effects=True, vmem_limit_bytes=40 * 1024 * 1024
            ),
        )(
            *(
                pltpu.with_memory_space_constraint(value, pltpu.MemorySpace.HBM)
                for value in (first_level, block_slot, cov_trail, factor_panel, factor_window, diag_inverse)
            )
        )

    return jax.shard_map(
        shards,
        mesh=mesh,
        in_specs=(P("prow", "pcol"), P(None, "prow", None), P(), P(), P(), P()),
        out_specs=(P(None, "prow", None), P()),
        check_vma=False,
    )
```
